256 devices in a mesh: rows: 32 (over z, y), irrep: 8 (over x, core).
Axes of the slice: x: 4, y: 4, z: 8, core: 2. Of those that a mesh axis runs over, the one named last changes fastest.
Arguments:
- coefficients: float32 [8, 2560, 2560], P('irrep', 'rows'), may hold values from -6 to 6
- block_codes: int32 [8, 4, 4, 320], P('irrep'), may hold values from -1 to 19, as said below
- tile_bank: float32 [8, 4, 8, 128, 128], P('irrep'), may hold values from -0.125 to 0.125
Outputs:
- sigma_vector: float32 [8, 2560, 2560], P('irrep', 'rows')
The draws below stay inside these ranges and needn't reach their ends.
Inputs may be any that keep to these rules, and one draw needn't show every extreme that they name: Fields 0 and 1 of block_codes[g, k] are block numbers below 20 for k = 0, 3 and below 20 for k = 1, 2; the first of them list the diagonal blocks 0, 1, ... in order, so every block row holds a listed block; field 2 is a tile number below 8; field 3 is -1 or +1.
All inputs are finite; a program needn't handle non-finite values.
Results may differ from the reference program's by a relative error of at most 0.0001.
Values sent between devices are 32-bit elements; how exact they have to be, the bound alone decides.
No kernel may reach another device: no remote copies, remote signals or barrier semaphores. Data moves between devices by JAX's collectives and lax.ppermute only.
A program may use at most 128 MiB of HBM per device.

```python
import jax
import jax.numpy as jnp
from jax import lax

NA = 2560
NB = 2560
BLK = 128
NNZ = 320
NT = 8
NIRR = 8


def draw_block_codes(key, part):
    base_key = jax.random.fold_in(key, 11)
    position = jnp.arange(NNZ, dtype=jnp.int32)[None, :]
    operators = []
    for which_op in range(4):
        op_key = jax.random.fold_in(base_key, which_op)
        keys_here = jax.random.split(op_key, 4)
        if which_op == 0 or which_op == 3:
            block_count = NB // BLK
        else:
            block_count = NA // BLK
        row_draw = jax.random.randint(keys_here[0], (NIRR, NNZ), 0, block_count, dtype=jnp.int32)
        col_draw = jax.random.randint(keys_here[1], (NIRR, NNZ), 0, block_count, dtype=jnp.int32)
        row_block = jnp.where(position < block_count, position, row_draw)
        col_block = jnp.where(position < block_count, position, col_draw)
        tile_index = jax.random.randint(keys_here[2], (NIRR, NNZ), 0, NT, dtype=jnp.int32)
        sign_draw = jax.random.randint(keys_here[3], (NIRR, NNZ), 0, 2, dtype=jnp.int32) * 2 - 1
        sign_value = jnp.where(position == 0, jnp.int32(-1), sign_draw)
        operators.append(jnp.stack([row_block, col_block, tile_index, sign_value], axis=1))
    return jnp.stack(operators, axis=1).astype(jnp.int32)


def levels(own_key, extent, cuts, smallest, high):
    gain = 1.0
    for axis_at, shards_of in cuts:
        steps = jax.random.uniform(jax.random.fold_in(jax.random.fold_in(own_key, 6), axis_at), (shards_of,), jnp.float32, smallest / len(cuts), high / len(cuts))
        gain = gain * jnp.repeat(jnp.exp(steps), extent[axis_at] // shards_of).reshape((-1,) + (1,) * (len(extent) - 1 - axis_at))
    return gain


def bell_draw(rng, extent, spread, bound, shards=(), kind=jnp.bfloat16):
    values = jax.random.normal(rng, extent, jnp.float32) * spread
    if len(shards) > 0:
        values = levels(rng, extent, shards, -0.22, 0.18) * values
    return jnp.clip(values, min=-bound, max=bound).astype(kind)


def setup_inputs(seed: int = 0) -> dict:
    streams_of = jax.random.split(jax.random.key(seed), 4)
    coefficients = bell_draw(streams_of[0], (NIRR, NA, NB), 1.0, 6.0, ((0, 8), (1, 32)), jnp.float32)
    block_codes = draw_block_codes(jax.random.fold_in(streams_of[3], 71), 0)
    tile_bank = bell_draw(streams_of[2], (NIRR, 4, NT, BLK, BLK), (NNZ * BLK * BLK // NB) ** -0.5, 0.125, ((0, 8),), jnp.float32)
    return dict(coefficients=coefficients, block_codes=block_codes, tile_bank=tile_bank)


highest = lax.Precision.HIGHEST


def apply_operator(values, block_codes, tile_bank):
    tile_size = tile_bank.shape[-1]
    tile_count = tile_bank.shape[0]
    block_count = values.shape[-1] // tile_size
    pieces = values.reshape(values.shape[0], block_count, tile_size)
    every_tile = jnp.einsum("rbq,tpq->rbtp", pieces, tile_bank, precision=highest)
    every_tile = every_tile.reshape(values.shape[0], block_count * tile_count, tile_size)
    flat_index = (block_codes[1] * tile_count + block_codes[2]).astype(jnp.int32)
    product = jnp.take(every_tile, flat_index, axis=1)
    placed = jnp.where(block_codes[0][:, None] == jnp.arange(block_count, dtype=jnp.int32)[None, :], block_codes[3][:, None].astype(jnp.float32), jnp.float32(0.0))
    result = jnp.einsum("rkp,kb->rbp", product, placed, precision=highest)
    return result.reshape(values.shape[0], block_count * tile_size)


def reference(coefficients, block_codes, tile_bank):
    outputs = []
    for irrep_index in range(NIRR):
        partner_index = (irrep_index + NIRR // 2) % NIRR
        own_block = coefficients[irrep_index]
        codes_here = block_codes[irrep_index]
        tiles_here = tile_bank[irrep_index]
        beta_term = apply_operator(own_block, codes_here[0], tiles_here[0])
        alpha_term = apply_operator(own_block.T, codes_here[1], tiles_here[1]).T
        mixed = apply_operator(coefficients[partner_index], codes_here[3], tiles_here[3])
        cross_term = apply_operator(mixed.T, codes_here[2], tiles_here[2]).T
        outputs.append(beta_term + alpha_term + cross_term)
    return jnp.stack(outputs)
```

```python
import functools

import jax
import jax.numpy as jnp
from jax import lax
from jax.experimental import pallas as pl
from jax.experimental.pallas import tpu as pltpu
from jax.sharding import PartitionSpec as P

LANES = 128
PACKED = 56
GROUP = 8
f32, bf16 = jnp.float32, jnp.bfloat16
VMEM, SMEM = pltpu.VMEM, pltpu.SMEM


def lane_of(rows):
    return lax.broadcasted_iota(jnp.int32, (rows, LANES), 1)


def rolled(value, shift):
    shift %= LANES
    return value if shift == 0 else pltpu.roll(value, shift, 1)


def pack(z):
    by32, by64, by80 = rolled(z[48:64], 32), rolled(z[64:80], 64), rolled(z[48:80], 80)
    top = jnp.where(lane_of(32) < 80, z[0:32], by80)
    middle = jnp.where(lane_of(16) < 80, z[32:48], jnp.where(lane_of(16) < 112, by32, by64))
    bottom = jnp.where(lane_of(8) < 16, by64[0:8], by80[24:32])
    return jnp.concatenate([top, middle, bottom], axis=0)


def unpack(p):
    by48 = rolled(p[0:32], 48)
    rows48 = jnp.where(lane_of(16) < 48, by48[0:16], rolled(p[32:48], 96))
    tail = rolled(p[32:48], 64)
    lane = lane_of(8)
    rows64 = jnp.where(lane < 48, by48[16:24], jnp.where(lane < 64, tail[0:8], rolled(p[48:56], 64)))
    rows72 = jnp.where(lane < 48, by48[24:32], jnp.where(lane < 64, tail[8:16], rolled(p[48:56], 48)))
    return jnp.concatenate([p[0:48], rows48, rows64, rows72], axis=0)


def send_transposed(tile_at, count, send_ref, turned_ref):
    rows = turned_ref.shape[0] // send_ref.shape[0]

    def turn(j, _):
        turned_ref[pl.ds(pl.multiple_of(j * LANES, LANES), LANES), 0:rows] = tile_at(j).T
        return 0

    lax.fori_loop(0, count, turn, 0)

    def one(d, _):
        send_ref[d] = pack(turned_ref[pl.ds(pl.multiple_of(d * rows, 8), rows), :])
        return 0

    lax.fori_loop(0, send_ref.shape[0], one, 0)


def split_into(lhs_ref, j, value):
    rows = value.shape[0]
    high = value.astype(bf16)
    low = (value - high.astype(f32)).astype(bf16)
    at = pl.ds(pl.multiple_of(j * rows, 16), rows)
    lhs_ref[at, 0:128] = high
    lhs_ref[at, 128:256] = low
    lhs_ref[at, 256:384] = high


def receive_rows(recv_ref, pieces_ref, lhs_ref):
    rows = pieces_ref.shape[1]

    def group(g, _):
        for c in range(GROUP):
            pieces_ref[c] = unpack(recv_ref[g * GROUP + c])
        for b in range(GROUP * rows // LANES):
            first, last = b * LANES // rows, (b * LANES + LANES - 1) // rows
            value = rolled(pieces_ref[last], last * rows - b * LANES)
            for c in range(last - 1, first - 1, -1):
                end = c * rows + rows - b * LANES
                value = jnp.where(
                    lane_of(rows) < end, rolled(pieces_ref[c], c * rows - b * LANES), value
                )
            split_into(lhs_ref, g * (GROUP * rows // LANES) + b, value)
        return 0

    lax.fori_loop(0, recv_ref.shape[0] // GROUP, group, 0)


def send_rows(sum_ref, send_ref):
    rows = sum_ref.shape[1]

    def group(g, _):
        base = g * (GROUP * rows // LANES)
        for c in range(GROUP):
            b, o = c * rows // LANES, c * rows % LANES
            value = rolled(sum_ref[base + b], -o)
            if o + rows > LANES:
                value = jnp.where(
                    lane_of(rows) < LANES - o, value, rolled(sum_ref[base + b + 1], -o)
                )
            send_ref[g * GROUP + c] = pack(value)
        return 0

    lax.fori_loop(0, send_ref.shape[0] // GROUP, group, 0)


def operate(which_op, codes_ref, weights_ref, lhs_ref, products_ref, sum_ref):
    rows = sum_ref.shape[1]
    wide = 2 * LANES

    def multiply(n, _):
        at = pl.ds(pl.multiple_of(n * wide, wide), wide)
        products_ref[:, at] = jnp.dot(
            lhs_ref[...], weights_ref[:, at], preferred_element_type=f32
        )
        return 0

    lax.fori_loop(0, weights_ref.shape[1] // wide, multiply, 0)

    def add(m, _):
        i, j = codes_ref[which_op, 0, m], codes_ref[which_op, 1, m]
        t, sign = codes_ref[which_op, 2, m], codes_ref[which_op, 3, m].astype(f32)
        product = products_ref[
            pl.ds(pl.multiple_of(j * rows, 8), rows), pl.ds(pl.multiple_of(t * LANES, LANES), LANES)
        ]
        sum_ref[i] += sign * product
        return 0

    lax.fori_loop(0, codes_ref.shape[2], add, 0, unroll=8)


def columns(ref, j):
    return ref[:, pl.ds(pl.multiple_of(j * LANES, LANES), LANES)]


def format_kernel(c_ref, send_ref, turned_ref):
    send_transposed(lambda j: columns(c_ref, j), c_ref.shape[1] // LANES, send_ref, turned_ref)


def weights_kernel(tiles_ref, weights_ref):
    def one(at, _):
        k, t = at // tiles_ref.shape[1], at % tiles_ref.shape[1]
        tile = tiles_ref[k, t].T
        high = tile.astype(bf16)
        low = (tile - high.astype(f32)).astype(bf16)
        lanes = pl.ds(pl.multiple_of(t * LANES, LANES), LANES)
        weights_ref[k, 0:128, lanes] = high
        weights_ref[k, 128:256, lanes] = high
        weights_ref[k, 256:384, lanes] = low
        return 0

    lax.fori_loop(0, tiles_ref.shape[0] * tiles_ref.shape[1], one, 0)


def split_all(c_ref, lhs_ref):
    def one(j, _):
        split_into(lhs_ref, j, columns(c_ref, j))
        return 0

    lax.fori_loop(0, c_ref.shape[1] // LANES, one, 0)


def beta_kernel(codes_ref, c_ref, weights_ref, sum_ref, lhs_ref, products_ref):
    split_all(c_ref, lhs_ref)
    sum_ref[...] = jnp.zeros_like(sum_ref)
    operate(0, codes_ref, weights_ref, lhs_ref, products_ref, sum_ref)


def mixed_kernel(codes_ref, c_ref, weights_ref, send_ref, lhs_ref, products_ref, sum_ref, turned_ref):
    split_all(c_ref, lhs_ref)
    sum_ref[...] = jnp.zeros_like(sum_ref)
    operate(3, codes_ref, weights_ref, lhs_ref, products_ref, sum_ref)
    send_transposed(lambda j: sum_ref[j], sum_ref.shape[0], send_ref, turned_ref)


def alpha_kernel(codes_ref, recv_ref, weights_ref, sum_ref, lhs_ref, products_ref, pieces_ref):
    receive_rows(recv_ref, pieces_ref, lhs_ref)
    sum_ref[...] = jnp.zeros_like(sum_ref)
    operate(1, codes_ref, weights_ref, lhs_ref, products_ref, sum_ref)


def cross_kernel(codes_ref, recv_ref, weights_ref, own_ref, send_ref, lhs_ref, products_ref, pieces_ref, sum_ref):
    receive_rows(recv_ref, pieces_ref, lhs_ref)
    sum_ref[...] = own_ref[...]
    operate(2, codes_ref, weights_ref, lhs_ref, products_ref, sum_ref)
    send_rows(sum_ref, send_ref)


def final_kernel(recv_ref, beta_ref, out_ref, turned_ref):
    rows = out_ref.shape[0]

    def one(d, _):
        turned_ref[pl.ds(pl.multiple_of(d * rows, 8), rows), :] = unpack(recv_ref[d])
        return 0

    lax.fori_loop(0, recv_ref.shape[0], one, 0)

    def turn(j, _):
        back = turned_ref[pl.ds(pl.multiple_of(j * LANES, LANES), LANES), :].T
        out_ref[:, pl.ds(pl.multiple_of(j * LANES, LANES), LANES)] = back[0:rows] + beta_ref[j]
        return 0

    lax.fori_loop(0, beta_ref.shape[0], turn, 0)


def call(kernel, out, scratch, operands, flops, name):
    specs = [
        pl.BlockSpec(memory_space=SMEM if x.dtype == jnp.int32 else VMEM) for x in operands
    ]
    moved = sum(x.size * x.dtype.itemsize for x in operands)
    return pl.pallas_call(
        kernel,
        out_shape=out,
        in_specs=specs,
        out_specs=pl.BlockSpec(memory_space=VMEM),
        scratch_shapes=scratch,
        compiler_params=pltpu.CompilerParams(vmem_limit_bytes=40 << 20),
        cost_estimate=pl.CostEstimate(flops=flops, bytes_accessed=moved, transcendentals=0),
        name=name,
    )(*operands)


def body(coefficients, block_codes, tile_bank):
    shards = lax.axis_size("rows")
    irreps = lax.axis_size("irrep")
    own, codes, tiles = coefficients[0], block_codes[0], tile_bank[0]
    rows, width = own.shape
    blocks, tile_count = width // LANES, tiles.shape[1]
    flops = 6 * rows * blocks * LANES * LANES * tile_count

    packed = jax.ShapeDtypeStruct((shards, PACKED, LANES), f32)
    summed = jax.ShapeDtypeStruct((blocks, rows, LANES), f32)
    lhs = VMEM((blocks * rows, 3 * LANES), bf16)
    products = VMEM((blocks * rows, tile_count * LANES), f32)
    turned = VMEM((width, LANES), f32)
    pieces = VMEM((GROUP, rows, LANES), f32)
    total = VMEM((blocks, rows, LANES), f32)

    def exchange(x):
        return lax.all_to_all(x, "rows", split_axis=0, concat_axis=0, tiled=True)

    partner = lax.ppermute(own, "irrep", [(i, i ^ irreps // 2) for i in range(irreps)])
    columns_in = exchange(call(format_kernel, packed, [turned], (own,), 1 << 20, "format"))
    weights = call(
        weights_kernel,
        jax.ShapeDtypeStruct((tiles.shape[0], 3 * LANES, tile_count * LANES), bf16),
        [],
        (tiles,),
        1 << 20,
        "weights",
    )
    mixed = call(
        mixed_kernel, packed, [lhs, products, total, turned], (codes, partner, weights[3]), flops, "mixed"
    )
    cross_in = exchange(mixed)
    beta = call(beta_kernel, summed, [lhs, products], (codes, own, weights[0]), flops, "beta")
    alpha = call(
        alpha_kernel, summed, [lhs, products, pieces], (codes, columns_in, weights[1]), flops, "alpha"
    )
    returned = exchange(
        call(
            cross_kernel,
            packed,
            [lhs, products, pieces, total],
            (codes, cross_in, weights[2], alpha),
            flops,
            "cross",
        )
    )
    out = call(
        final_kernel, jax.ShapeDtypeStruct((rows, width), f32), [turned], (returned, beta), 1 << 20, "final"
    )
    return out[None]


def solution(mesh):
    in_specs = (
        P("irrep", "rows", None),
        P("irrep", None, None, None),
        P("irrep", None, None, None, None),
    )
    out_specs = P("irrep", "rows", None)
    return jax.shard_map(body, mesh=mesh, in_specs=in_specs, out_specs=out_specs, check_vma=False)
```

```python
import jax
import jax.numpy as jnp
from jax import lax
from jax.experimental import pallas as pl
from jax.experimental.pallas import tpu as pltpu
from jax.sharding import PartitionSpec as P


LANES = 128
PACKED = 56
GROUP = 8
RUN = 8
f32, bf16 = jnp.float32, jnp.bfloat16
VMEM, SMEM = pltpu.VMEM, pltpu.SMEM


def lane_of(rows):
    return lax.broadcasted_iota(jnp.int32, (rows, LANES), 1)


def rolled(value, shift):
    shift %= LANES
    return value if shift == 0 else pltpu.roll(value, shift, 1)


def pack(z):
    by32, by64, by80 = rolled(z[48:64], 32), rolled(z[64:80], 64), rolled(z[48:80], 80)
    top = jnp.where(lane_of(32) < 80, z[0:32], by80)
    middle = jnp.where(lane_of(16) < 80, z[32:48], jnp.where(lane_of(16) < 112, by32, by64))
    bottom = jnp.where(lane_of(8) < 16, by64[0:8], by80[24:32])
    return jnp.concatenate([top, middle, bottom], axis=0)


def unpack(p):
    by48 = rolled(p[0:32], 48)
    rows48 = jnp.where(lane_of(16) < 48, by48[0:16], rolled(p[32:48], 96))
    tail = rolled(p[32:48], 64)
    lane = lane_of(8)
    rows64 = jnp.where(lane < 48, by48[16:24], jnp.where(lane < 64, tail[0:8], rolled(p[48:56], 64)))
    rows72 = jnp.where(lane < 48, by48[24:32], jnp.where(lane < 64, tail[8:16], rolled(p[48:56], 48)))
    return jnp.concatenate([p[0:48], rows48, rows64, rows72], axis=0)


def send_transposed(tile_at, count, send_ref, turned_ref):
    rows = turned_ref.shape[0] // send_ref.shape[0]

    def turn(j, _):
        turned_ref[pl.ds(pl.multiple_of(j * LANES, LANES), LANES), 0:rows] = tile_at(j).T
        return 0

    lax.fori_loop(0, count, turn, 0, unroll=5)

    def one(d, _):
        send_ref[d] = pack(turned_ref[pl.ds(pl.multiple_of(d * rows, 8), rows), :])
        return 0

    lax.fori_loop(0, send_ref.shape[0], one, 0, unroll=4)


def split_into(lhs_ref, j, value):
    rows = value.shape[0]
    high = value.astype(bf16)
    low = (value - high.astype(f32)).astype(bf16)
    at = pl.ds(pl.multiple_of(j * rows, 16), rows)
    lhs_ref[at, 0:128] = high
    lhs_ref[at, 128:256] = low
    lhs_ref[at, 256:384] = high


def receive_rows(recv_ref, pieces_ref, lhs_ref):
    rows = pieces_ref.shape[1]

    def group(g, _):
        for c in range(GROUP):
            pieces_ref[c] = unpack(recv_ref[g * GROUP + c])
        for b in range(GROUP * rows // LANES):
            first, last = b * LANES // rows, (b * LANES + LANES - 1) // rows
            value = rolled(pieces_ref[last], last * rows - b * LANES)
            for c in range(last - 1, first - 1, -1):
                end = c * rows + rows - b * LANES
                value = jnp.where(
                    lane_of(rows) < end, rolled(pieces_ref[c], c * rows - b * LANES), value
                )
            split_into(lhs_ref, g * (GROUP * rows // LANES) + b, value)
        return 0

    lax.fori_loop(0, recv_ref.shape[0] // GROUP, group, 0)


def send_rows(sum_ref, send_ref):
    rows = sum_ref.shape[1]

    def group(g, _):
        base = g * (GROUP * rows // LANES)
        for c in range(GROUP):
            b, o = c * rows // LANES, c * rows % LANES
            value = rolled(sum_ref[base + b], -o)
            if o + rows > LANES:
                value = jnp.where(
                    lane_of(rows) < LANES - o, value, rolled(sum_ref[base + b + 1], -o)
                )
            send_ref[g * GROUP + c] = pack(value)
        return 0

    lax.fori_loop(0, send_ref.shape[0] // GROUP, group, 0)


def operate(which_op, words_ref, starts_ref, weights_ref, lhs_ref, products_ref, sum_ref, first):
    blocks, rows, _ = sum_ref.shape
    tile_count = products_ref.shape[0] // blocks

    def multiply(n, _):
        at = pl.ds(pl.multiple_of(n * 2 * LANES, 2 * LANES), 2 * LANES)
        both = jnp.dot(lhs_ref[...], weights_ref[:, at], preferred_element_type=f32)
        for j in range(blocks):
            for half in range(2):
                products_ref[j * tile_count + 2 * n + half] = both[
                    j * rows : (j + 1) * rows, half * LANES : (half + 1) * LANES
                ]
        return 0

    lax.fori_loop(0, tile_count // 2, multiply, 0)

    def output_block(i, _):
        def run(q, total):
            for u in range(RUN):
                word = words_ref[which_op, q * RUN + u]
                sign = ((word & 1) - ((word >> 1) & 1)).astype(f32)
                total = total + sign * products_ref[word >> 2]
            return total

        sum_ref[i] = lax.fori_loop(
            starts_ref[which_op, i], starts_ref[which_op, i + 1], run, first(i)
        )
        return 0

    lax.fori_loop(0, blocks, output_block, 0)


def runs_of(block_codes, blocks, tile_count):
    row, column, tile, sign = (block_codes[:, field] for field in range(4))
    words = (column * tile_count + tile) * 4 + jnp.where(sign > 0, 1, 2)
    listed = row.shape[1]
    slots = (listed + blocks * (RUN - 1) + 127) // 128 * 128
    at = jnp.arange(listed, dtype=jnp.int32)
    block = jnp.arange(blocks, dtype=jnp.int32)
    within = jnp.sum(
        (row[:, None, :] == row[:, :, None]) & (at[None, None, :] < at[None, :, None]),
        axis=2,
        dtype=jnp.int32,
    )
    counts = jnp.sum(row[:, None, :] == block[None, :, None], axis=2, dtype=jnp.int32)
    runs = (counts + RUN - 1) // RUN
    begin = jnp.sum(jnp.where(block[None, None, :] < row[:, :, None], runs[:, None, :], 0), axis=2)
    place = begin * RUN + within
    slot = jnp.arange(slots, dtype=jnp.int32)
    grouped = jnp.sum(
        jnp.where(place[:, None, :] == slot[None, :, None], words[:, None, :], 0), axis=2
    )
    bound = jnp.arange(blocks + 1, dtype=jnp.int32)
    starts = jnp.sum(jnp.where(block[None, None, :] < bound[None, :, None], runs[:, None, :], 0), axis=2)
    return grouped.astype(jnp.int32), starts.astype(jnp.int32)


def columns(ref, j):
    return ref[:, pl.ds(pl.multiple_of(j * LANES, LANES), LANES)]


def format_kernel(c_ref, send_ref, turned_ref):
    send_transposed(lambda j: columns(c_ref, j), c_ref.shape[1] // LANES, send_ref, turned_ref)


def weights_kernel(tiles_ref, *weights_refs):
    for k, weights_ref in enumerate(weights_refs):

        def one(t, _):
            tile = tiles_ref[k, t].T
            high = tile.astype(bf16)
            low = (tile - high.astype(f32)).astype(bf16)
            lanes = pl.ds(pl.multiple_of(t * LANES, LANES), LANES)
            weights_ref[0:128, lanes] = high
            weights_ref[128:256, lanes] = high
            weights_ref[256:384, lanes] = low
            return 0

        lax.fori_loop(0, tiles_ref.shape[1], one, 0, unroll=2)


def split_all(c_ref, lhs_ref):
    def one(j, _):
        split_into(lhs_ref, j, columns(c_ref, j))
        return 0

    lax.fori_loop(0, c_ref.shape[1] // LANES, one, 0, unroll=4)


def zeros_like_block(ref):
    return lambda i: jnp.zeros(ref.shape[1:], f32)


def beta_kernel(words_ref, starts_ref, c_ref, weights_ref, sum_ref, lhs_ref, products_ref):
    split_all(c_ref, lhs_ref)
    operate(0, words_ref, starts_ref, weights_ref, lhs_ref, products_ref, sum_ref, zeros_like_block(sum_ref))


def mixed_kernel(words_ref, starts_ref, c_ref, weights_ref, send_ref, lhs_ref, products_ref, sum_ref, turned_ref):
    split_all(c_ref, lhs_ref)
    operate(3, words_ref, starts_ref, weights_ref, lhs_ref, products_ref, sum_ref, zeros_like_block(sum_ref))
    send_transposed(lambda j: sum_ref[j], sum_ref.shape[0], send_ref, turned_ref)


def alpha_kernel(words_ref, starts_ref, recv_ref, weights_ref, sum_ref, lhs_ref, products_ref, pieces_ref):
    receive_rows(recv_ref, pieces_ref, lhs_ref)
    operate(1, words_ref, starts_ref, weights_ref, lhs_ref, products_ref, sum_ref, zeros_like_block(sum_ref))


def cross_kernel(
    words_ref, starts_ref, recv_ref, weights_ref, own_ref, send_ref, lhs_ref, products_ref, pieces_ref, sum_ref
):
    receive_rows(recv_ref, pieces_ref, lhs_ref)
    operate(2, words_ref, starts_ref, weights_ref, lhs_ref, products_ref, sum_ref, lambda i: own_ref[i])
    send_rows(sum_ref, send_ref)


def final_kernel(recv_ref, beta_ref, out_ref, turned_ref):
    rows = out_ref.shape[0]

    def one(d, _):
        turned_ref[pl.ds(pl.multiple_of(d * rows, 8), rows), :] = unpack(recv_ref[d])
        return 0

    lax.fori_loop(0, recv_ref.shape[0], one, 0, unroll=4)

    def turn(j, _):
        back = turned_ref[pl.ds(pl.multiple_of(j * LANES, LANES), LANES), :].T
        out_ref[:, pl.ds(pl.multiple_of(j * LANES, LANES), LANES)] = back[0:rows] + beta_ref[j]
        return 0

    lax.fori_loop(0, beta_ref.shape[0], turn, 0, unroll=5)


def call(kernel, out, scratch, operands, flops):
    specs = [
        pl.BlockSpec(memory_space=SMEM if x.dtype == jnp.int32 else VMEM) for x in operands
    ]
    moved = sum(x.size * x.dtype.itemsize for x in operands)
    return pl.pallas_call(
        kernel,
        out_shape=out,
        in_specs=specs,
        out_specs=jax.tree.map(lambda _: pl.BlockSpec(memory_space=VMEM), out),
        scratch_shapes=scratch,
        compiler_params=pltpu.CompilerParams(vmem_limit_bytes=20 << 20),
        cost_estimate=pl.CostEstimate(flops=flops, bytes_accessed=moved, transcendentals=0),
    )(*operands)


def steps(coefficients, block_codes, tile_bank):
    shards = lax.axis_size("rows")
    irreps = lax.axis_size("irrep")
    own, codes, tiles = coefficients[0], block_codes[0], tile_bank[0]
    rows, width = own.shape
    blocks, tile_count = width // LANES, tiles.shape[1]
    flops = 6 * rows * blocks * LANES * LANES * tile_count

    packed = jax.ShapeDtypeStruct((shards, PACKED, LANES), f32)
    summed = jax.ShapeDtypeStruct((blocks, rows, LANES), f32)
    lhs = VMEM((blocks * rows, 3 * LANES), bf16)
    products = VMEM((blocks * tile_count, rows, LANES), f32)
    turned = VMEM((width, LANES), f32)
    pieces = VMEM((GROUP, rows, LANES), f32)
    total = VMEM((blocks, rows, LANES), f32)
    weights = jax.ShapeDtypeStruct((3 * LANES, tile_count * LANES), bf16)

    def exchange(x):
        return lax.all_to_all(x, "rows", split_axis=0, concat_axis=0, tiled=True)

    partner = lax.ppermute(own, "irrep", [(i, i ^ irreps // 2) for i in range(irreps)])
    listed = runs_of(codes, blocks, tile_count)
    columns_in = exchange(call(format_kernel, packed, [turned], (own,), 1 << 20))
    w0, w1, w2, w3 = call(weights_kernel, [weights] * tiles.shape[0], [], (tiles,), 1 << 20)
    mixed = call(mixed_kernel, packed, [lhs, products, total, turned], (*listed, partner, w3), flops)
    cross_in = exchange(mixed)
    beta = call(beta_kernel, summed, [lhs, products], (*listed, own, w0), flops)
    alpha = call(alpha_kernel, summed, [lhs, products, pieces], (*listed, columns_in, w1), flops)
    cross = call(cross_kernel, packed, [lhs, products, pieces, total], (*listed, cross_in, w2, alpha), flops)
    returned = exchange(cross)
    out = call(final_kernel, jax.ShapeDtypeStruct((rows, width), f32), [turned], (returned, beta), 1 << 20)
    return out[None]


def solution(mesh):
    in_specs = (
        P("irrep", "rows", None),
        P("irrep", None, None, None),
        P("irrep", None, None, None, None),
    )
    out_specs = P("irrep", "rows", None)
    return jax.shard_map(steps, mesh=mesh, in_specs=in_specs, out_specs=out_specs, check_vma=False)
```

```python
import jax
import jax.numpy as jnp
from jax import lax
from jax.experimental import pallas as pl
from jax.experimental.pallas import tpu as pltpu
from jax.sharding import PartitionSpec as P


LANES = 128
PACKED = 50
GROUP = 8
RUN = 8
f32, bf16 = jnp.float32, jnp.bfloat16
VMEM, SMEM = pltpu.VMEM, pltpu.SMEM


def lane_of(rows):
    return lax.broadcasted_iota(jnp.int32, (rows, LANES), 1)


def rolled(value, shift):
    shift %= LANES
    return value if shift == 0 else pltpu.roll(value, shift, 1)


CORNER = 16


def sublane():
    return lax.broadcasted_iota(jnp.int32, (8, LANES), 0)


def put(send_ref, d, z):
    by32, by64, by80 = rolled(z[48:64], 32), rolled(z[64:80], 64), rolled(z[48:80], 80)
    send_ref[pl.ds(d * PACKED, 32), :] = jnp.where(lane_of(32) < 80, z[0:32], by80)
    send_ref[pl.ds(d * PACKED + 32, 16), :] = jnp.where(
        lane_of(16) < 80, z[32:48], jnp.where(lane_of(16) < 112, by32, by64)
    )
    for a in range(2):
        slanted = pltpu.roll(by64[8 * a : 8 * a + 8], 0, 1, stride=CORNER, stride_axis=0)
        send_ref[pl.ds(d * PACKED + 48 + a, 1), :] = jnp.sum(
            jnp.where(lane_of(8) // CORNER == sublane(), slanted, 0.0), axis=0, keepdims=True
        )


def get(recv_ref, s):
    p = recv_ref[pl.ds(s * PACKED, 48), :]
    by48 = rolled(p[0:32], 48)
    rows48 = jnp.where(lane_of(16) < 48, by48[0:16], rolled(p[32:48], 96))
    tail = rolled(p[32:48], 64)
    lane = lane_of(8)
    last = []
    for a in range(2):
        line = jnp.broadcast_to(recv_ref[pl.ds(s * PACKED + 48 + a, 1), :], (8, LANES))
        corner = rolled(line, 64)
        for bit in (1, 2, 4):
            corner = jnp.where(sublane() & bit > 0, rolled(corner, -bit * CORNER), corner)
        at = slice(8 * a, 8 * a + 8)
        last.append(
            jnp.where(lane < 48, by48[16 + 8 * a : 24 + 8 * a], jnp.where(lane < 64, tail[at], corner))
        )
    return jnp.concatenate([p[0:48], rows48, *last], axis=0)


def send_transposed(tile_at, count, send_ref, turned_ref):
    shards = send_ref.shape[0] // PACKED
    rows = turned_ref.shape[0] // shards

    def turn(j, _):
        turned_ref[pl.ds(pl.multiple_of(j * LANES, LANES), LANES), 0:rows] = tile_at(j).T
        return 0

    lax.fori_loop(0, count, turn, 0, unroll=5)

    def one(d, _):
        put(send_ref, d, turned_ref[pl.ds(pl.multiple_of(d * rows, 8), rows), :])
        return 0

    lax.fori_loop(0, shards, one, 0, unroll=4)


def split_into(lhs_ref, j, value):
    rows = value.shape[0]
    high = value.astype(bf16)
    low = (value - high.astype(f32)).astype(bf16)
    at = pl.ds(pl.multiple_of(j * rows, 16), rows)
    lhs_ref[at, 0:128] = high
    lhs_ref[at, 128:256] = low
    lhs_ref[at, 256:384] = high


def receive_rows(recv_ref, pieces_ref, lhs_ref):
    rows = pieces_ref.shape[1]

    def group(g, _):
        for c in range(GROUP):
            pieces_ref[c] = get(recv_ref, g * GROUP + c)
        for b in range(GROUP * rows // LANES):
            first, last = b * LANES // rows, (b * LANES + LANES - 1) // rows
            value = rolled(pieces_ref[last], last * rows - b * LANES)
            for c in range(last - 1, first - 1, -1):
                end = c * rows + rows - b * LANES
                value = jnp.where(
                    lane_of(rows) < end, rolled(pieces_ref[c], c * rows - b * LANES), value
                )
            split_into(lhs_ref, g * (GROUP * rows // LANES) + b, value)
        return 0

    lax.fori_loop(0, recv_ref.shape[0] // PACKED // GROUP, group, 0)


def send_rows(sum_ref, send_ref):
    rows = sum_ref.shape[1]

    def group(g, _):
        base = g * (GROUP * rows // LANES)
        for c in range(GROUP):
            b, o = c * rows // LANES, c * rows % LANES
            value = rolled(sum_ref[base + b], -o)
            if o + rows > LANES:
                value = jnp.where(
                    lane_of(rows) < LANES - o, value, rolled(sum_ref[base + b + 1], -o)
                )
            put(send_ref, g * GROUP + c, value)
        return 0

    lax.fori_loop(0, send_ref.shape[0] // PACKED // GROUP, group, 0)


def operate(which_op, words_ref, starts_ref, weights_ref, lhs_ref, products_ref, sum_ref, first):
    blocks, rows, _ = sum_ref.shape
    tile_count = products_ref.shape[0] // blocks

    def multiply(n, _):
        at = pl.ds(pl.multiple_of(n * 2 * LANES, 2 * LANES), 2 * LANES)
        both = jnp.dot(lhs_ref[...], weights_ref[:, at], preferred_element_type=f32)
        for j in range(blocks):
            for half in range(2):
                products_ref[j * tile_count + 2 * n + half] = both[
                    j * rows : (j + 1) * rows, half * LANES : (half + 1) * LANES
                ]
        return 0

    lax.fori_loop(0, tile_count // 2, multiply, 0)

    def output_block(i, _):
        def run(q, total):
            for u in range(RUN):
                word = words_ref[which_op, q * RUN + u]
                sign = ((word & 1) - ((word >> 1) & 1)).astype(f32)
                total = total + sign * products_ref[word >> 2]
            return total

        sum_ref[i] = lax.fori_loop(
            starts_ref[which_op, i], starts_ref[which_op, i + 1], run, first(i)
        )
        return 0

    lax.fori_loop(0, blocks, output_block, 0)


def runs_of(block_codes, blocks, tile_count):
    row, column, tile, sign = (block_codes[:, field] for field in range(4))
    words = (column * tile_count + tile) * 4 + jnp.where(sign > 0, 1, 2)
    listed = row.shape[1]
    slots = (listed + blocks * (RUN - 1) + 127) // 128 * 128
    at = jnp.arange(listed, dtype=jnp.int32)
    block = jnp.arange(blocks, dtype=jnp.int32)
    within = jnp.sum(
        (row[:, None, :] == row[:, :, None]) & (at[None, None, :] < at[None, :, None]),
        axis=2,
        dtype=jnp.int32,
    )
    counts = jnp.sum(row[:, None, :] == block[None, :, None], axis=2, dtype=jnp.int32)
    runs = (counts + RUN - 1) // RUN
    begin = jnp.sum(jnp.where(block[None, None, :] < row[:, :, None], runs[:, None, :], 0), axis=2)
    place = begin * RUN + within
    slot = jnp.arange(slots, dtype=jnp.int32)
    grouped = jnp.sum(
        jnp.where(place[:, None, :] == slot[None, :, None], words[:, None, :], 0), axis=2
    )
    bound = jnp.arange(blocks + 1, dtype=jnp.int32)
    starts = jnp.sum(jnp.where(block[None, None, :] < bound[None, :, None], runs[:, None, :], 0), axis=2)
    return grouped.astype(jnp.int32), starts.astype(jnp.int32)


def columns(ref, j):
    return ref[:, pl.ds(pl.multiple_of(j * LANES, LANES), LANES)]


def format_kernel(c_ref, send_ref, turned_ref):
    send_transposed(lambda j: columns(c_ref, j), c_ref.shape[1] // LANES, send_ref, turned_ref)


def weights_kernel(tiles_ref, *weights_refs):
    for k, weights_ref in enumerate(weights_refs):

        def one(t, _):
            tile = tiles_ref[k, t].T
            high = tile.astype(bf16)
            low = (tile - high.astype(f32)).astype(bf16)
            lanes = pl.ds(pl.multiple_of(t * LANES, LANES), LANES)
            weights_ref[0:128, lanes] = high
            weights_ref[128:256, lanes] = high
            weights_ref[256:384, lanes] = low
            return 0

        lax.fori_loop(0, tiles_ref.shape[1], one, 0, unroll=2)


def split_all(c_ref, lhs_ref):
    def one(j, _):
        split_into(lhs_ref, j, columns(c_ref, j))
        return 0

    lax.fori_loop(0, c_ref.shape[1] // LANES, one, 0, unroll=4)


def zeros_like_block(ref):
    return lambda i: jnp.zeros(ref.shape[1:], f32)


def beta_kernel(words_ref, starts_ref, c_ref, w_ref, sum_ref, lhs_ref, products_ref, weights_ref, sem):
    fetch = pltpu.make_async_copy(w_ref, weights_ref, sem)
    fetch.start()
    split_all(c_ref, lhs_ref)
    fetch.wait()
    operate(0, words_ref, starts_ref, weights_ref, lhs_ref, products_ref, sum_ref, zeros_like_block(sum_ref))


def mixed_kernel(
    words_ref, starts_ref, c_ref, w_ref, send_ref, lhs_ref, products_ref, weights_ref, sem, sum_ref, turned_ref
):
    fetch = pltpu.make_async_copy(w_ref, weights_ref, sem)
    fetch.start()
    split_all(c_ref, lhs_ref)
    fetch.wait()
    operate(3, words_ref, starts_ref, weights_ref, lhs_ref, products_ref, sum_ref, zeros_like_block(sum_ref))
    send_transposed(lambda j: sum_ref[j], sum_ref.shape[0], send_ref, turned_ref)


def alpha_kernel(
    words_ref, starts_ref, recv_ref, w_ref, sum_ref, lhs_ref, products_ref, weights_ref, sem, pieces_ref
):
    fetch = pltpu.make_async_copy(w_ref, weights_ref, sem)
    fetch.start()
    receive_rows(recv_ref, pieces_ref, lhs_ref)
    fetch.wait()
    operate(1, words_ref, starts_ref, weights_ref, lhs_ref, products_ref, sum_ref, zeros_like_block(sum_ref))


def cross_kernel(
    words_ref,
    starts_ref,
    recv_ref,
    w_ref,
    alpha_ref,
    send_ref,
    lhs_ref,
    products_ref,
    weights_ref,
    sem,
    pieces_ref,
    sum_ref,
    own_ref,
    own_sem,
):
    fetch = pltpu.make_async_copy(w_ref, weights_ref, sem)
    fetch.start()
    fetch_own = pltpu.make_async_copy(alpha_ref, own_ref, own_sem)
    fetch_own.start()
    receive_rows(recv_ref, pieces_ref, lhs_ref)
    fetch.wait()
    fetch_own.wait()
    operate(2, words_ref, starts_ref, weights_ref, lhs_ref, products_ref, sum_ref, lambda i: own_ref[i])
    send_rows(sum_ref, send_ref)


def final_kernel(recv_ref, beta_ref, out_ref, turned_ref):
    rows = out_ref.shape[0]

    def one(d, _):
        turned_ref[pl.ds(pl.multiple_of(d * rows, 8), rows), :] = get(recv_ref, d)
        return 0

    lax.fori_loop(0, recv_ref.shape[0] // PACKED, one, 0, unroll=4)

    def turn(j, _):
        back = turned_ref[pl.ds(pl.multiple_of(j * LANES, LANES), LANES), :].T
        out_ref[:, pl.ds(pl.multiple_of(j * LANES, LANES), LANES)] = back[0:rows] + beta_ref[j]
        return 0

    lax.fori_loop(0, beta_ref.shape[0], turn, 0, unroll=5)


def call(kernel, out, scratch, operands, flops, fetched=()):
    specs = [
        pl.BlockSpec(
            memory_space=SMEM if x.dtype == jnp.int32 else pl.ANY if at in fetched else VMEM
        )
        for at, x in enumerate(operands)
    ]
    moved = sum(x.size * x.dtype.itemsize for x in operands)
    return pl.pallas_call(
        kernel,
        out_shape=out,
        in_specs=specs,
        out_specs=jax.tree.map(lambda _: pl.BlockSpec(memory_space=VMEM), out),
        scratch_shapes=scratch,
        compiler_params=pltpu.CompilerParams(vmem_limit_bytes=52 << 20),
        cost_estimate=pl.CostEstimate(flops=flops, bytes_accessed=moved, transcendentals=0),
    )(*operands)


def steps(coefficients, block_codes, tile_bank):
    shards = lax.axis_size("rows")
    irreps = lax.axis_size("irrep")
    own, codes, tiles = coefficients[0], block_codes[0], tile_bank[0]
    rows, width = own.shape
    blocks, tile_count = width // LANES, tiles.shape[1]
    flops = 6 * rows * blocks * LANES * LANES * tile_count

    packed = jax.ShapeDtypeStruct((shards * PACKED, LANES), f32)
    summed = jax.ShapeDtypeStruct((blocks, rows, LANES), f32)
    lhs = VMEM((blocks * rows, 3 * LANES), bf16)
    products = VMEM((blocks * tile_count, rows, LANES), f32)
    turned = VMEM((width, LANES), f32)
    pieces = VMEM((GROUP, rows, LANES), f32)
    total = VMEM((blocks, rows, LANES), f32)
    work = [lhs, products, VMEM((3 * LANES, tile_count * LANES), bf16), pltpu.SemaphoreType.DMA]
    weights = jax.ShapeDtypeStruct((3 * LANES, tile_count * LANES), bf16)

    def exchange(x):
        x = x.reshape(shards, PACKED // 2, 2, LANES)
        x = lax.all_to_all(x, "rows", split_axis=0, concat_axis=0, tiled=True)
        return x.reshape(shards * PACKED, LANES)

    partner = lax.ppermute(own, "irrep", [(i, i ^ irreps // 2) for i in range(irreps)])
    listed = runs_of(codes, blocks, tile_count)
    columns_in = exchange(call(format_kernel, packed, [turned], (own,), 1 << 20))
    w0, w1, w2, w3 = call(weights_kernel, [weights] * tiles.shape[0], [], (tiles,), 1 << 20)
    mixed = call(mixed_kernel, packed, [*work, total, turned], (*listed, partner, w3), flops, (3,))
    cross_in = exchange(mixed)
    beta = call(beta_kernel, summed, work, (*listed, own, w0), flops, (3,))
    alpha = call(alpha_kernel, summed, [*work, pieces], (*listed, columns_in, w1), flops, (3,))
    cross = call(
        cross_kernel,
        packed,
        [*work, pieces, total, total, pltpu.SemaphoreType.DMA],
        (*listed, cross_in, w2, alpha),
        flops,
        (3, 4),
    )
    returned = exchange(cross)
    out = call(final_kernel, jax.ShapeDtypeStruct((rows, width), f32), [turned], (returned, beta), 1 << 20)
    return out[None]


def solution(mesh):
    in_specs = (
        P("irrep", "rows", None),
        P("irrep", None, None, None),
        P("irrep", None, None, None, None),
    )
    out_specs = P("irrep", "rows", None)
    return jax.shard_map(steps, mesh=mesh, in_specs=in_specs, out_specs=out_specs, check_vma=False)
```

```python
import jax
import jax.numpy as jnp
from jax import lax
from jax.experimental import pallas as pl
from jax.experimental.pallas import tpu as pltpu
from jax.sharding import PartitionSpec as P


LANES = 128
PACKED = 50
GROUP = 8
RUN = 8
TOGETHER = 2
f32, bf16 = jnp.float32, jnp.bfloat16
VMEM, SMEM = pltpu.VMEM, pltpu.SMEM


def lane_of(rows):
    return lax.broadcasted_iota(jnp.int32, (rows, LANES), 1)


def rolled(value, shift):
    shift %= LANES
    return value if shift == 0 else pltpu.roll(value, shift, 1)


CORNER = 16


def sublane():
    return lax.broadcasted_iota(jnp.int32, (8, LANES), 0)


def put(send_ref, d, z):
    by32, by64, by80 = rolled(z[48:64], 32), rolled(z[64:80], 64), rolled(z[48:80], 80)
    send_ref[pl.ds(d * PACKED, 32), :] = jnp.where(lane_of(32) < 80, z[0:32], by80)
    send_ref[pl.ds(d * PACKED + 32, 16), :] = jnp.where(
        lane_of(16) < 80, z[32:48], jnp.where(lane_of(16) < 112, by32, by64)
    )
    lane = lane_of(8)
    corner = jnp.where(lane < 16, by64[0:8], by80[24:32])
    corner = jnp.where(lane < 32, corner, rolled(pltpu.roll(corner, 4, 0), 32))
    corner = jnp.where(lane < 64, corner, rolled(pltpu.roll(corner, 6, 0), 64))
    send_ref[pl.ds(d * PACKED + 48, 2), :] = corner[0:2]


def get(recv_ref, s):
    p = recv_ref[pl.ds(s * PACKED, 48), :]
    by48 = rolled(p[0:32], 48)
    rows48 = jnp.where(lane_of(16) < 48, by48[0:16], rolled(p[32:48], 96))
    tail = rolled(p[32:48], 64)
    two = recv_ref[pl.ds(s * PACKED + 48, 2), :]
    corner = jnp.concatenate([two, two, two, two], axis=0)
    lane = lane_of(8)
    corner = jnp.where(sublane() & 2 > 0, rolled(corner, 64), corner)
    corner = jnp.where(sublane() & 4 > 0, rolled(corner, 96), corner)
    last = []
    for a in range(2):
        at = slice(8 * a, 8 * a + 8)
        last.append(
            jnp.where(
                lane < 48,
                by48[16 + 8 * a : 24 + 8 * a],
                jnp.where(lane < 64, tail[at], rolled(corner, 64 - CORNER * a)),
            )
        )
    return jnp.concatenate([p[0:48], rows48, *last], axis=0)


def send_transposed(tile_at, count, send_ref, turned_ref):
    rows = turned_ref.shape[0] * PACKED // send_ref.shape[0]

    def turn(j, _):
        turned_ref[pl.ds(pl.multiple_of(j * LANES, LANES), LANES), 0:rows] = tile_at(j).T
        return 0

    lax.fori_loop(0, count, turn, 0, unroll=5)
    send_turned(send_ref, turned_ref)


def send_turned(send_ref, turned_ref):
    shards = send_ref.shape[0] // PACKED
    rows = turned_ref.shape[0] // shards

    def one(d, _):
        put(send_ref, d, turned_ref[pl.ds(pl.multiple_of(d * rows, 8), rows), :])
        return 0

    lax.fori_loop(0, shards, one, 0, unroll=8)


def split_into(lhs_ref, j, value):
    rows = value.shape[0]
    high = value.astype(bf16)
    low = (value - high.astype(f32)).astype(bf16)
    at = pl.ds(pl.multiple_of(j * rows, 16), rows)
    lhs_ref[at, 0:128] = high
    lhs_ref[at, 128:256] = low
    lhs_ref[at, 256:384] = high


def receive_rows(recv_ref, pieces_ref, lhs_ref):
    rows = pieces_ref.shape[1]

    def group(g, _):
        for c in range(GROUP):
            pieces_ref[c] = get(recv_ref, g * GROUP + c)
        for b in range(GROUP * rows // LANES):
            first, last = b * LANES // rows, (b * LANES + LANES - 1) // rows
            value = rolled(pieces_ref[last], last * rows - b * LANES)
            for c in range(last - 1, first - 1, -1):
                end = c * rows + rows - b * LANES
                value = jnp.where(
                    lane_of(rows) < end, rolled(pieces_ref[c], c * rows - b * LANES), value
                )
            split_into(lhs_ref, g * (GROUP * rows // LANES) + b, value)
        return 0

    lax.fori_loop(0, recv_ref.shape[0] // PACKED // GROUP, group, 0)


def send_rows(sum_ref, send_ref):
    rows = sum_ref.shape[1]

    def group(g, _):
        base = g * (GROUP * rows // LANES)
        for c in range(GROUP):
            b, o = c * rows // LANES, c * rows % LANES
            value = rolled(sum_ref[base + b], -o)
            if o + rows > LANES:
                value = jnp.where(
                    lane_of(rows) < LANES - o, value, rolled(sum_ref[base + b + 1], -o)
                )
            put(send_ref, g * GROUP + c, value)
        return 0

    lax.fori_loop(0, send_ref.shape[0] // PACKED // GROUP, group, 0)


def operate(lists, weights_ref, lhs_ref, products_ref, sum_ref, first):
    blocks, rows, _ = sum_ref.shape
    tile_count = products_ref.shape[0] // blocks
    numbers_ref, signs_ref = lists.wait()

    def multiply(n, _):
        at = pl.ds(pl.multiple_of(n * 2 * LANES, 2 * LANES), 2 * LANES)
        both = jnp.dot(lhs_ref[...], weights_ref[:, at], preferred_element_type=f32)
        for j in range(blocks):
            for half in range(2):
                products_ref[j * tile_count + 2 * n + half] = both[
                    j * rows : (j + 1) * rows, half * LANES : (half + 1) * LANES
                ]
        return 0

    lax.fori_loop(0, tile_count // 2, multiply, 0)
    for i in range(blocks):
        sum_ref[i] = first(i)
    slots = signs_ref.shape[0]

    def run(q, _):
        added = []
        for r in range(TOGETHER):
            at = (q * TOGETHER + r) * RUN
            total = signs_ref[at] * products_ref[numbers_ref[at]]
            for u in range(1, RUN):
                total = total + signs_ref[at + u] * products_ref[numbers_ref[at + u]]
            added.append(total)
        for r in range(TOGETHER):
            sum_ref[numbers_ref[slots + q * TOGETHER + r]] += added[r]
        return 0

    runs = numbers_ref[slots + slots // RUN]
    lax.fori_loop(0, (runs + TOGETHER - 1) // TOGETHER, run, 0)


def runs_of(block_codes, blocks, tile_count):
    row, column, tile, sign = (block_codes[:, field] for field in range(4))
    words = ((column * tile_count + tile) * blocks + row) * 4 + jnp.where(sign > 0, 1, 2)
    listed = row.shape[1]
    slots = (listed + blocks * (RUN - 1) + (TOGETHER - 1) * RUN + 127) // 128 * 128
    at = jnp.arange(listed, dtype=jnp.int32)
    block = jnp.arange(blocks, dtype=jnp.int32)
    within = jnp.sum(
        (row[:, None, :] == row[:, :, None]) & (at[None, None, :] < at[None, :, None]),
        axis=2,
        dtype=jnp.int32,
    )
    counts = jnp.sum(row[:, None, :] == block[None, :, None], axis=2, dtype=jnp.int32)
    runs = (counts + RUN - 1) // RUN
    begin = jnp.sum(jnp.where(block[None, None, :] < row[:, :, None], runs[:, None, :], 0), axis=2)
    place = begin * RUN + within
    slot = jnp.arange(slots, dtype=jnp.int32)
    grouped = jnp.sum(
        jnp.where(place[:, None, :] == slot[None, :, None], words[:, None, :], 0), axis=2
    )
    signs = ((grouped & 1) - ((grouped >> 1) & 1)).astype(f32)
    pair = grouped >> 2
    targets = (pair % blocks).reshape(pair.shape[0], slots // RUN, RUN)[:, :, 0]
    all_runs = jnp.sum(runs, axis=1, keepdims=True)
    numbers = jnp.concatenate([pair // blocks, targets, all_runs], axis=1)
    numbers = jnp.pad(numbers, ((0, 0), (0, -numbers.shape[1] % LANES)))
    return numbers.astype(jnp.int32), signs


class Lists:
    def __init__(self, which_op, given, held, sems):
        self.held = held
        self.copies = [
            pltpu.make_async_copy(source.at[which_op], target, sems.at[at])
            for at, (source, target) in enumerate(zip(given, held))
        ]
        for copy in self.copies:
            copy.start()

    def wait(self):
        for copy in self.copies:
            copy.wait()
        return self.held


def columns(ref, j):
    return ref[:, pl.ds(pl.multiple_of(j * LANES, LANES), LANES)]


def format_kernel(c_ref, send_ref, held_ref, sems, turned_ref):
    parts = sems.shape[0]
    width = c_ref.shape[1] // parts
    copies = [
        pltpu.make_async_copy(
            c_ref.at[:, part * width : (part + 1) * width],
            held_ref.at[:, part * width : (part + 1) * width],
            sems.at[part],
        )
        for part in range(parts)
    ]
    for copy in copies:
        copy.start()
    rows = held_ref.shape[0]
    for part in range(parts):
        copies[part].wait()
        for j in range(part * width // LANES, (part + 1) * width // LANES):
            lanes = slice(j * LANES, (j + 1) * LANES)
            turned_ref[lanes, 0:rows] = held_ref[:, lanes].T
    send_turned(send_ref, turned_ref)


def weights_kernel(tiles_ref, *weights_refs):
    for k, weights_ref in enumerate(weights_refs):

        def one(t, _):
            tile = tiles_ref[k, t].T
            high = tile.astype(bf16)
            low = (tile - high.astype(f32)).astype(bf16)
            lanes = pl.ds(pl.multiple_of(t * LANES, LANES), LANES)
            weights_ref[0:128, lanes] = high
            weights_ref[128:256, lanes] = high
            weights_ref[256:384, lanes] = low
            return 0

        lax.fori_loop(0, tiles_ref.shape[1], one, 0, unroll=2)


def split_all(c_ref, lhs_ref):
    def one(j, _):
        split_into(lhs_ref, j, columns(c_ref, j))
        return 0

    lax.fori_loop(0, c_ref.shape[1] // LANES, one, 0, unroll=4)


def zeros_like_block(ref):
    return lambda i: jnp.zeros(ref.shape[1:], f32)


def beta_kernel(n_ref, s_ref, c_ref, w_ref, sum_ref, *work):
    lhs_ref, products_ref, weights_ref, sem, numbers_ref, signs_ref, sems = work
    fetch = pltpu.make_async_copy(w_ref, weights_ref, sem)
    fetch.start()
    lists = Lists(0, (n_ref, s_ref), (numbers_ref, signs_ref), sems)
    split_all(c_ref, lhs_ref)
    fetch.wait()
    operate(lists, weights_ref, lhs_ref, products_ref, sum_ref, zeros_like_block(sum_ref))


def mixed_kernel(n_ref, s_ref, c_ref, w_ref, send_ref, *work):
    lhs_ref, products_ref, weights_ref, sem, numbers_ref, signs_ref, sems, sum_ref, turned_ref = work
    fetch = pltpu.make_async_copy(w_ref, weights_ref, sem)
    fetch.start()
    lists = Lists(3, (n_ref, s_ref), (numbers_ref, signs_ref), sems)
    split_all(c_ref, lhs_ref)
    fetch.wait()
    operate(lists, weights_ref, lhs_ref, products_ref, sum_ref, zeros_like_block(sum_ref))
    send_transposed(lambda j: sum_ref[j], sum_ref.shape[0], send_ref, turned_ref)


def alpha_kernel(n_ref, s_ref, recv_ref, w_ref, sum_ref, *work):
    lhs_ref, products_ref, weights_ref, sem, numbers_ref, signs_ref, sems, pieces_ref = work
    fetch = pltpu.make_async_copy(w_ref, weights_ref, sem)
    fetch.start()
    lists = Lists(1, (n_ref, s_ref), (numbers_ref, signs_ref), sems)
    receive_rows(recv_ref, pieces_ref, lhs_ref)
    fetch.wait()
    operate(lists, weights_ref, lhs_ref, products_ref, sum_ref, zeros_like_block(sum_ref))


def cross_kernel(n_ref, s_ref, recv_ref, w_ref, alpha_ref, send_ref, *work):
    lhs_ref, products_ref, weights_ref, sem, numbers_ref, signs_ref, sems, *rest = work
    pieces_ref, sum_ref, own_ref, own_sem = rest
    fetch = pltpu.make_async_copy(w_ref, weights_ref, sem)
    fetch.start()
    fetch_own = pltpu.make_async_copy(alpha_ref, own_ref, own_sem)
    fetch_own.start()
    lists = Lists(2, (n_ref, s_ref), (numbers_ref, signs_ref), sems)
    receive_rows(recv_ref, pieces_ref, lhs_ref)
    fetch.wait()
    fetch_own.wait()
    operate(lists, weights_ref, lhs_ref, products_ref, sum_ref, lambda i: own_ref[i])
    send_rows(sum_ref, send_ref)


def final_kernel(recv_ref, b_ref, o_ref, turned_ref, beta_ref, sem, out_ref, sems):
    rows = out_ref.shape[0]
    fetch = pltpu.make_async_copy(b_ref, beta_ref, sem)
    fetch.start()

    def one(d, _):
        turned_ref[pl.ds(pl.multiple_of(d * rows, 8), rows), :] = get(recv_ref, d)
        return 0

    lax.fori_loop(0, recv_ref.shape[0] // PACKED, one, 0, unroll=8)
    fetch.wait()
    parts = sems.shape[0]
    width = out_ref.shape[1] // parts
    copies = []
    for part in range(parts):
        for j in range(part * width // LANES, (part + 1) * width // LANES):
            lanes = slice(j * LANES, (j + 1) * LANES)
            out_ref[:, lanes] = turned_ref[lanes, :].T[0:rows] + beta_ref[j]
        at = slice(part * width, (part + 1) * width)
        copies.append(pltpu.make_async_copy(out_ref.at[:, at], o_ref.at[:, at], sems.at[part]))
        copies[-1].start()
    for copy in copies:
        copy.wait()


def call(kernel, out, scratch, operands, flops, held=(), out_space=VMEM, room=52):
    specs = [
        pl.BlockSpec(memory_space=VMEM if at in held else pl.ANY) for at, x in enumerate(operands)
    ]
    moved = sum(x.size * x.dtype.itemsize for x in operands)
    return pl.pallas_call(
        kernel,
        out_shape=out,
        in_specs=specs,
        out_specs=jax.tree.map(lambda _: pl.BlockSpec(memory_space=out_space), out),
        scratch_shapes=scratch,
        compiler_params=pltpu.CompilerParams(vmem_limit_bytes=room << 20),
        cost_estimate=pl.CostEstimate(flops=flops, bytes_accessed=moved, transcendentals=0),
    )(*operands)


def steps(coefficients, block_codes, tile_bank):
    shards = lax.axis_size("rows")
    irreps = lax.axis_size("irrep")
    own, codes, tiles = coefficients[0], block_codes[0], tile_bank[0]
    rows, width = own.shape
    blocks, tile_count = width // LANES, tiles.shape[1]
    flops = 6 * rows * blocks * LANES * LANES * tile_count

    packed = jax.ShapeDtypeStruct((shards * PACKED, LANES), f32)
    summed = jax.ShapeDtypeStruct((blocks, rows, LANES), f32)
    weights = jax.ShapeDtypeStruct((3 * LANES, tile_count * LANES), bf16)
    numbers, signs = runs_of(codes, blocks, tile_count)
    turned = VMEM((width, LANES), f32)
    pieces = VMEM((GROUP, rows, LANES), f32)
    total = VMEM((blocks, rows, LANES), f32)
    whole = VMEM((rows, width), f32)
    dma = pltpu.SemaphoreType.DMA
    parts = 5
    work = [
        VMEM((blocks * rows, 3 * LANES), bf16),
        VMEM((blocks * tile_count, rows, LANES), f32),
        VMEM(weights.shape, bf16),
        dma,
        SMEM(numbers.shape[1:], jnp.int32),
        SMEM(signs.shape[1:], f32),
        dma((2,)),
    ]

    def exchange(x):
        x = x.reshape(shards, PACKED // 2, 2, LANES)
        x = lax.all_to_all(x, "rows", split_axis=0, concat_axis=0, tiled=True)
        return x.reshape(shards * PACKED, LANES)

    partner = lax.ppermute(own, "irrep", [(i, i ^ irreps // 2) for i in range(irreps)])
    formatted = call(
        format_kernel, packed, [whole, dma((parts,)), turned], (own,), 1 << 20, room=60
    )
    columns_in = exchange(formatted)
    w0, w1, w2, w3 = call(weights_kernel, [weights] * tiles.shape[0], [], (tiles,), 1 << 20, (0,))
    lists = (numbers, signs)
    mixed = call(mixed_kernel, packed, [*work, total, turned], (*lists, partner, w3), flops, (2,))
    cross_in = exchange(mixed)
    beta = call(beta_kernel, summed, work, (*lists, own, w0), flops, (2,))
    alpha = call(alpha_kernel, summed, [*work, pieces], (*lists, columns_in, w1), flops, (2,))
    cross = call(
        cross_kernel,
        packed,
        [*work, pieces, total, total, dma],
        (*lists, cross_in, w2, alpha),
        flops,
        (2,),
    )
    returned = exchange(cross)
    out = call(
        final_kernel,
        jax.ShapeDtypeStruct((rows, width), f32),
        [turned, total, dma, whole, dma((parts,))],
        (returned, beta),
        1 << 20,
        (0,),
        pl.ANY,
    )
    return out[None]


def solution(mesh):
    in_specs = (
        P("irrep", "rows", None),
        P("irrep", None, None, None),
        P("irrep", None, None, None, None),
    )
    out_specs = P("irrep", "rows", None)
    return jax.shard_map(steps, mesh=mesh, in_specs=in_specs, out_specs=out_specs, check_vma=False)
```

```python
import jax
import jax.numpy as jnp
from jax import lax
from jax.experimental import pallas as pl
from jax.experimental.pallas import tpu as pltpu
from jax.sharding import PartitionSpec as P


LANES = 128
PACKED = 50
GROUP = 8
RUN = 8
TOGETHER = 2
f32, bf16 = jnp.float32, jnp.bfloat16
VMEM, SMEM = pltpu.VMEM, pltpu.SMEM


def lane_of(rows):
    return lax.broadcasted_iota(jnp.int32, (rows, LANES), 1)


def rolled(value, shift):
    shift %= LANES
    return value if shift == 0 else pltpu.roll(value, shift, 1)


CORNER = 16


def sublane():
    return lax.broadcasted_iota(jnp.int32, (8, LANES), 0)


def put(send_ref, d, z):
    by32, by64, by80 = rolled(z[48:64], 32), rolled(z[64:80], 64), rolled(z[48:80], 80)
    send_ref[pl.ds(d * PACKED, 32), :] = jnp.where(lane_of(32) < 80, z[0:32], by80)
    send_ref[pl.ds(d * PACKED + 32, 16), :] = jnp.where(
        lane_of(16) < 80, z[32:48], jnp.where(lane_of(16) < 112, by32, by64)
    )
    lane = lane_of(8)
    corner = jnp.where(lane < 16, by64[0:8], by80[24:32])
    corner = jnp.where(lane < 32, corner, rolled(pltpu.roll(corner, 4, 0), 32))
    corner = jnp.where(lane < 64, corner, rolled(pltpu.roll(corner, 6, 0), 64))
    send_ref[pl.ds(d * PACKED + 48, 2), :] = corner[0:2]


def get(recv_ref, s):
    p = recv_ref[pl.ds(s * PACKED, 48), :]
    by48 = rolled(p[0:32], 48)
    rows48 = jnp.where(lane_of(16) < 48, by48[0:16], rolled(p[32:48], 96))
    tail = rolled(p[32:48], 64)
    two = recv_ref[pl.ds(s * PACKED + 48, 2), :]
    corner = jnp.concatenate([two, two, two, two], axis=0)
    lane = lane_of(8)
    corner = jnp.where(sublane() & 2 > 0, rolled(corner, 64), corner)
    corner = jnp.where(sublane() & 4 > 0, rolled(corner, 96), corner)
    last = []
    for a in range(2):
        at = slice(8 * a, 8 * a + 8)
        last.append(
            jnp.where(
                lane < 48,
                by48[16 + 8 * a : 24 + 8 * a],
                jnp.where(lane < 64, tail[at], rolled(corner, 64 - CORNER * a)),
            )
        )
    return jnp.concatenate([p[0:48], rows48, *last], axis=0)


def send_transposed(tile_at, count, out, turned_ref):
    rows = turned_ref.shape[0] * PACKED // out[1].shape[0]

    def turn(j, _):
        turned_ref[pl.ds(pl.multiple_of(j * LANES, LANES), LANES), 0:rows] = tile_at(j).T
        return 0

    lax.fori_loop(0, count, turn, 0, unroll=10)
    send_turned(out, turned_ref)


def send_turned(out, turned_ref):
    o_ref, send_ref, sems = out
    halves = sems.shape[0]
    shards = send_ref.shape[0] // PACKED
    rows = turned_ref.shape[0] // shards
    each = shards // halves

    def copy_of(h):
        at = pl.ds(pl.multiple_of(h * each * PACKED, 8), each * PACKED)
        return pltpu.make_async_copy(send_ref.at[at], o_ref.at[at], sems.at[h])

    def half(h, _):
        for c in range(each):
            d = h * each + c
            put(send_ref, d, turned_ref[pl.ds(pl.multiple_of(d * rows, 8), rows), :])
        copy_of(h).start()
        return 0

    lax.fori_loop(0, halves, half, 0)
    for h in range(halves):
        copy_of(h).wait()


def split_into(lhs_ref, j, value):
    rows = value.shape[0]
    high = value.astype(bf16)
    low = (value - high.astype(f32)).astype(bf16)
    at = pl.ds(pl.multiple_of(j * rows, 16), rows)
    lhs_ref[at, 0:128] = high
    lhs_ref[at, 128:256] = low
    lhs_ref[at, 256:384] = high


def receive_rows(recv_ref, pieces_ref, lhs_ref):
    rows = pieces_ref.shape[1]

    def group(g, _):
        for c in range(GROUP):
            pieces_ref[c] = get(recv_ref, g * GROUP + c)
        for b in range(GROUP * rows // LANES):
            first, last = b * LANES // rows, (b * LANES + LANES - 1) // rows
            value = rolled(pieces_ref[last], last * rows - b * LANES)
            for c in range(last - 1, first - 1, -1):
                end = c * rows + rows - b * LANES
                value = jnp.where(
                    lane_of(rows) < end, rolled(pieces_ref[c], c * rows - b * LANES), value
                )
            split_into(lhs_ref, g * (GROUP * rows // LANES) + b, value)
        return 0

    lax.fori_loop(0, recv_ref.shape[0] // PACKED // GROUP, group, 0)


def send_rows(sum_ref, out, turned_ref):
    rows = sum_ref.shape[1]

    def group(g, _):
        base = g * (GROUP * rows // LANES)
        for c in range(GROUP):
            b, o = c * rows // LANES, c * rows % LANES
            value = rolled(sum_ref[base + b], -o)
            if o + rows > LANES:
                value = jnp.where(
                    lane_of(rows) < LANES - o, value, rolled(sum_ref[base + b + 1], -o)
                )
            turned_ref[pl.ds(pl.multiple_of((g * GROUP + c) * rows, 8), rows), :] = value
        return 0

    lax.fori_loop(0, turned_ref.shape[0] // rows // GROUP, group, 0)
    send_turned(out, turned_ref)


def operate(lists, weights_ref, lhs_ref, products_ref, sum_ref):
    blocks, rows, _ = sum_ref.shape
    tile_count = products_ref.shape[0] // blocks
    numbers_ref, signs_ref = lists.wait()

    def multiply(n, _):
        at = pl.ds(pl.multiple_of(n * 2 * LANES, 2 * LANES), 2 * LANES)
        both = jnp.dot(lhs_ref[...], weights_ref[:, at], preferred_element_type=f32)
        for j in range(blocks):
            for half in range(2):
                products_ref[j * tile_count + 2 * n + half] = both[
                    j * rows : (j + 1) * rows, half * LANES : (half + 1) * LANES
                ]
        return 0

    lax.fori_loop(0, tile_count // 2, multiply, 0)
    slots = signs_ref.shape[0]

    def run(q, _):
        added = []
        for r in range(TOGETHER):
            at = (q * TOGETHER + r) * RUN
            total = signs_ref[at] * products_ref[numbers_ref[at]]
            for u in range(1, RUN):
                total = total + signs_ref[at + u] * products_ref[numbers_ref[at + u]]
            added.append(total)
        for r in range(TOGETHER):
            sum_ref[numbers_ref[slots + q * TOGETHER + r]] += added[r]
        return 0

    runs = numbers_ref[slots + slots // RUN]
    lax.fori_loop(0, (runs + TOGETHER - 1) // TOGETHER, run, 0)


def runs_of(block_codes, blocks, tile_count):
    row, column, tile, sign = (block_codes[:, field] for field in range(4))
    words = ((column * tile_count + tile) * blocks + row) * 4 + jnp.where(sign > 0, 1, 2)
    listed = row.shape[1]
    slots = (listed + blocks * (RUN - 1) + (TOGETHER - 1) * RUN + 127) // 128 * 128
    at = jnp.arange(listed, dtype=jnp.int32)
    block = jnp.arange(blocks, dtype=jnp.int32)
    within = jnp.sum(
        (row[:, None, :] == row[:, :, None]) & (at[None, None, :] < at[None, :, None]),
        axis=2,
        dtype=jnp.int32,
    )
    counts = jnp.sum(row[:, None, :] == block[None, :, None], axis=2, dtype=jnp.int32)
    runs = (counts + RUN - 1) // RUN
    begin = jnp.sum(jnp.where(block[None, None, :] < row[:, :, None], runs[:, None, :], 0), axis=2)
    place = begin * RUN + within
    slot = jnp.arange(slots, dtype=jnp.int32)
    grouped = jnp.sum(
        jnp.where(place[:, None, :] == slot[None, :, None], words[:, None, :], 0), axis=2
    )
    signs = ((grouped & 1) - ((grouped >> 1) & 1)).astype(f32)
    pair = grouped >> 2
    targets = (pair % blocks).reshape(pair.shape[0], slots // RUN, RUN)[:, :, 0]
    all_runs = jnp.sum(runs, axis=1, keepdims=True)
    numbers = jnp.concatenate([pair // blocks, targets, all_runs], axis=1)
    numbers = jnp.pad(numbers, ((0, 0), (0, -numbers.shape[1] % LANES)))
    return numbers.astype(jnp.int32), signs


class Lists:
    def __init__(self, which_op, given, held, sems):
        self.held = held
        self.copies = [
            pltpu.make_async_copy(source.at[which_op], target, sems.at[at])
            for at, (source, target) in enumerate(zip(given, held))
        ]
        for copy in self.copies:
            copy.start()

    def wait(self):
        for copy in self.copies:
            copy.wait()
        return self.held


def columns(ref, j):
    return ref[:, pl.ds(pl.multiple_of(j * LANES, LANES), LANES)]


def format_kernel(c_ref, o_ref, held_ref, sems, turned_ref, *buffer):
    parts = sems.shape[0]
    width = c_ref.shape[1] // parts
    copies = [
        pltpu.make_async_copy(
            c_ref.at[:, part * width : (part + 1) * width],
            held_ref.at[:, part * width : (part + 1) * width],
            sems.at[part],
        )
        for part in range(parts)
    ]
    for copy in copies:
        copy.start()
    rows = held_ref.shape[0]
    for part in range(parts):
        copies[part].wait()
        for j in range(part * width // LANES, (part + 1) * width // LANES):
            lanes = slice(j * LANES, (j + 1) * LANES)
            turned_ref[lanes, 0:rows] = held_ref[:, lanes].T
    send_turned((o_ref, *buffer), turned_ref)


def weights_kernel(tiles_ref, *weights_refs):
    for k, weights_ref in enumerate(weights_refs):

        def one(t, _):
            tile = tiles_ref[k, t].T
            high = tile.astype(bf16)
            low = (tile - high.astype(f32)).astype(bf16)
            lanes = pl.ds(pl.multiple_of(t * LANES, LANES), LANES)
            weights_ref[0:128, lanes] = high
            weights_ref[128:256, lanes] = high
            weights_ref[256:384, lanes] = low
            return 0

        lax.fori_loop(0, tiles_ref.shape[1], one, 0, unroll=2)


def split_all(c_ref, lhs_ref):
    def one(j, _):
        split_into(lhs_ref, j, columns(c_ref, j))
        return 0

    lax.fori_loop(0, c_ref.shape[1] // LANES, one, 0, unroll=4)


def beta_kernel(n_ref, s_ref, c_ref, w_ref, sum_ref, *work):
    lhs_ref, products_ref, weights_ref, sem, numbers_ref, signs_ref, sems = work
    fetch = pltpu.make_async_copy(w_ref, weights_ref, sem)
    fetch.start()
    lists = Lists(0, (n_ref, s_ref), (numbers_ref, signs_ref), sems)
    split_all(c_ref, lhs_ref)
    fetch.wait()
    sum_ref[...] = jnp.zeros_like(sum_ref)
    operate(lists, weights_ref, lhs_ref, products_ref, sum_ref)


def mixed_kernel(n_ref, s_ref, c_ref, w_ref, o_ref, *work):
    lhs_ref, products_ref, weights_ref, sem, numbers_ref, signs_ref, sems, *rest = work
    sum_ref, turned_ref, *buffer = rest
    fetch = pltpu.make_async_copy(w_ref, weights_ref, sem)
    fetch.start()
    lists = Lists(3, (n_ref, s_ref), (numbers_ref, signs_ref), sems)
    split_all(c_ref, lhs_ref)
    fetch.wait()
    sum_ref[...] = jnp.zeros_like(sum_ref)
    operate(lists, weights_ref, lhs_ref, products_ref, sum_ref)
    send_transposed(lambda j: sum_ref[j], sum_ref.shape[0], (o_ref, *buffer), turned_ref)


def alpha_kernel(n_ref, s_ref, recv_ref, w_ref, sum_ref, *work):
    lhs_ref, products_ref, weights_ref, sem, numbers_ref, signs_ref, sems, pieces_ref = work
    fetch = pltpu.make_async_copy(w_ref, weights_ref, sem)
    fetch.start()
    lists = Lists(1, (n_ref, s_ref), (numbers_ref, signs_ref), sems)
    receive_rows(recv_ref, pieces_ref, lhs_ref)
    fetch.wait()
    sum_ref[...] = jnp.zeros_like(sum_ref)
    operate(lists, weights_ref, lhs_ref, products_ref, sum_ref)


def cross_kernel(n_ref, s_ref, recv_ref, w_ref, alpha_ref, o_ref, *work):
    lhs_ref, products_ref, weights_ref, sem, numbers_ref, signs_ref, sems, *rest = work
    pieces_ref, sum_ref, own_sem, turned_ref, *buffer = rest
    fetch = pltpu.make_async_copy(w_ref, weights_ref, sem)
    fetch.start()
    fetch_own = pltpu.make_async_copy(alpha_ref, sum_ref, own_sem)
    fetch_own.start()
    lists = Lists(2, (n_ref, s_ref), (numbers_ref, signs_ref), sems)
    receive_rows(recv_ref, pieces_ref, lhs_ref)
    fetch.wait()
    fetch_own.wait()
    operate(lists, weights_ref, lhs_ref, products_ref, sum_ref)
    send_rows(sum_ref, (o_ref, *buffer), turned_ref)


def final_kernel(recv_ref, b_ref, o_ref, turned_ref, beta_ref, sem, out_ref, sems):
    rows = out_ref.shape[0]
    fetch = pltpu.make_async_copy(b_ref, beta_ref, sem)
    fetch.start()

    def one(d, _):
        turned_ref[pl.ds(pl.multiple_of(d * rows, 8), rows), :] = get(recv_ref, d)
        return 0

    lax.fori_loop(0, recv_ref.shape[0] // PACKED, one, 0, unroll=16)
    fetch.wait()
    parts = sems.shape[0]
    width = out_ref.shape[1] // parts
    copies = []
    for part in range(parts):
        for j in range(part * width // LANES, (part + 1) * width // LANES):
            lanes = slice(j * LANES, (j + 1) * LANES)
            out_ref[:, lanes] = turned_ref[lanes, :].T[0:rows] + beta_ref[j]
        at = slice(part * width, (part + 1) * width)
        copies.append(pltpu.make_async_copy(out_ref.at[:, at], o_ref.at[:, at], sems.at[part]))
        copies[-1].start()
    for copy in copies:
        copy.wait()


def call(kernel, out, scratch, operands, flops, held=(), out_space=VMEM, room=52):
    specs = [
        pl.BlockSpec(memory_space=VMEM if at in held else pl.ANY) for at, x in enumerate(operands)
    ]
    moved = sum(x.size * x.dtype.itemsize for x in operands)
    return pl.pallas_call(
        kernel,
        out_shape=out,
        in_specs=specs,
        out_specs=jax.tree.map(lambda _: pl.BlockSpec(memory_space=out_space), out),
        scratch_shapes=scratch,
        compiler_params=pltpu.CompilerParams(vmem_limit_bytes=room << 20),
        cost_estimate=pl.CostEstimate(flops=flops, bytes_accessed=moved, transcendentals=0),
    )(*operands)


def steps(coefficients, block_codes, tile_bank):
    shards = lax.axis_size("rows")
    irreps = lax.axis_size("irrep")
    own, codes, tiles = coefficients[0], block_codes[0], tile_bank[0]
    rows, width = own.shape
    blocks, tile_count = width // LANES, tiles.shape[1]
    flops = 6 * rows * blocks * LANES * LANES * tile_count

    packed = jax.ShapeDtypeStruct((shards * PACKED, LANES), f32)
    summed = jax.ShapeDtypeStruct((blocks, rows, LANES), f32)
    weights = jax.ShapeDtypeStruct((3 * LANES, tile_count * LANES), bf16)
    numbers, signs = runs_of(codes, blocks, tile_count)
    turned = VMEM((width, LANES), f32)
    pieces = VMEM((GROUP, rows, LANES), f32)
    total = VMEM((blocks, rows, LANES), f32)
    whole = VMEM((rows, width), f32)
    dma = pltpu.SemaphoreType.DMA
    parts = 5
    buffer = [VMEM(packed.shape, f32), dma((2,))]
    work = [
        VMEM((blocks * rows, 3 * LANES), bf16),
        VMEM((blocks * tile_count, rows, LANES), f32),
        VMEM(weights.shape, bf16),
        dma,
        SMEM(numbers.shape[1:], jnp.int32),
        SMEM(signs.shape[1:], f32),
        dma((2,)),
    ]

    def exchange(x):
        x = x.reshape(shards, PACKED // 2, 2, LANES)
        x = lax.all_to_all(x, "rows", split_axis=0, concat_axis=0, tiled=True)
        return x.reshape(shards * PACKED, LANES)

    partner = lax.ppermute(own, "irrep", [(i, i ^ irreps // 2) for i in range(irreps)])
    formatted = call(
        format_kernel,
        packed,
        [whole, dma((parts,)), turned, *buffer],
        (own,),
        1 << 20,
        out_space=pl.ANY,
        room=60,
    )
    columns_in = exchange(formatted)
    w0, w1, w2, w3 = call(weights_kernel, [weights] * tiles.shape[0], [], (tiles,), 1 << 20, (0,))
    lists = (numbers, signs)
    mixed = call(
        mixed_kernel,
        packed,
        [*work, total, turned, *buffer],
        (*lists, partner, w3),
        flops,
        (2,),
        pl.ANY,
    )
    cross_in = exchange(mixed)
    beta = call(beta_kernel, summed, work, (*lists, own, w0), flops, (2,))
    alpha = call(alpha_kernel, summed, [*work, pieces], (*lists, columns_in, w1), flops, (2,))
    cross = call(
        cross_kernel,
        packed,
        [*work, pieces, total, dma, turned, *buffer],
        (*lists, cross_in, w2, alpha),
        flops,
        (2,),
        pl.ANY,
    )
    returned = exchange(cross)
    out = call(
        final_kernel,
        jax.ShapeDtypeStruct((rows, width), f32),
        [turned, total, dma, whole, dma((parts,))],
        (returned, beta),
        1 << 20,
        (0,),
        pl.ANY,
    )
    return out[None]


def solution(mesh):
    in_specs = (
        P("irrep", "rows", None),
        P("irrep", None, None, None),
        P("irrep", None, None, None, None),
    )
    out_specs = P("irrep", "rows", None)
    return jax.shard_map(steps, mesh=mesh, in_specs=in_specs, out_specs=out_specs, check_vma=False)
```

```python
import jax
import jax.numpy as jnp
from jax import lax
from jax.experimental import pallas as pl
from jax.experimental.pallas import tpu as pltpu
from jax.sharding import PartitionSpec as P


LANES = 128
PACKED = 50
GROUP = 8
RUN = 8
TOGETHER = 2
f32, bf16 = jnp.float32, jnp.bfloat16
VMEM, SMEM = pltpu.VMEM, pltpu.SMEM


def lane_of(rows):
    return lax.broadcasted_iota(jnp.int32, (rows, LANES), 1)


def rolled(value, shift):
    shift %= LANES
    return value if shift == 0 else pltpu.roll(value, shift, 1)


CORNER = 16


def sublane():
    return lax.broadcasted_iota(jnp.int32, (8, LANES), 0)


def put(send_ref, d, z):
    by32, by64, by80 = rolled(z[48:64], 32), rolled(z[64:80], 64), rolled(z[48:80], 80)
    send_ref[pl.ds(d * PACKED, 32), :] = jnp.where(lane_of(32) < 80, z[0:32], by80)
    send_ref[pl.ds(d * PACKED + 32, 16), :] = jnp.where(
        lane_of(16) < 80, z[32:48], jnp.where(lane_of(16) < 112, by32, by64)
    )
    lane = lane_of(8)
    corner = jnp.where(lane < 16, by64[0:8], by80[24:32])
    corner = jnp.where(lane < 32, corner, rolled(pltpu.roll(corner, 4, 0), 32))
    corner = jnp.where(lane < 64, corner, rolled(pltpu.roll(corner, 6, 0), 64))
    send_ref[pl.ds(d * PACKED + 48, 2), :] = corner[0:2]


def get(recv_ref, s):
    p = recv_ref[pl.ds(s * PACKED, 48), :]
    by48 = rolled(p[0:32], 48)
    rows48 = jnp.where(lane_of(16) < 48, by48[0:16], rolled(p[32:48], 96))
    tail = rolled(p[32:48], 64)
    two = recv_ref[pl.ds(s * PACKED + 48, 2), :]
    corner = jnp.concatenate([two, two, two, two], axis=0)
    lane = lane_of(8)
    corner = jnp.where(sublane() & 2 > 0, rolled(corner, 64), corner)
    corner = jnp.where(sublane() & 4 > 0, rolled(corner, 96), corner)
    last = []
    for a in range(2):
        at = slice(8 * a, 8 * a + 8)
        last.append(
            jnp.where(
                lane < 48,
                by48[16 + 8 * a : 24 + 8 * a],
                jnp.where(lane < 64, tail[at], rolled(corner, 64 - CORNER * a)),
            )
        )
    return jnp.concatenate([p[0:48], rows48, *last], axis=0)


def send_transposed(tile_at, count, out, turned_ref):
    rows = turned_ref.shape[0] * PACKED // out[1].shape[0]

    def turn(j, _):
        turned_ref[pl.ds(pl.multiple_of(j * LANES, LANES), LANES), 0:rows] = tile_at(j).T
        return 0

    lax.fori_loop(0, count, turn, 0, unroll=10)
    send_turned(out, turned_ref)


def send_turned(out, turned_ref):
    o_ref, send_ref, sems = out
    halves = sems.shape[0]
    shards = send_ref.shape[0] // PACKED
    rows = turned_ref.shape[0] // shards
    each = shards // halves

    def copy_of(h):
        at = pl.ds(pl.multiple_of(h * each * PACKED, 8), each * PACKED)
        return pltpu.make_async_copy(send_ref.at[at], o_ref.at[at], sems.at[h])

    def half(h, _):
        for c in range(each):
            d = h * each + c
            put(send_ref, d, turned_ref[pl.ds(pl.multiple_of(d * rows, 8), rows), :])
        copy_of(h).start()
        return 0

    lax.fori_loop(0, halves, half, 0)
    for h in range(halves):
        copy_of(h).wait()


def split_into(lhs_ref, j, value):
    rows = value.shape[0]
    high = value.astype(bf16)
    low = (value - high.astype(f32)).astype(bf16)
    at = pl.ds(pl.multiple_of(j * rows, 16), rows)
    lhs_ref[at, 0:128] = high
    lhs_ref[at, 128:256] = low
    lhs_ref[at, 256:384] = high


def receive_rows(recv_ref, pieces_ref, lhs_ref):
    rows = pieces_ref.shape[1]

    def group(g, _):
        for c in range(GROUP):
            pieces_ref[c] = get(recv_ref, g * GROUP + c)
        for b in range(GROUP * rows // LANES):
            first, last = b * LANES // rows, (b * LANES + LANES - 1) // rows
            value = rolled(pieces_ref[last], last * rows - b * LANES)
            for c in range(last - 1, first - 1, -1):
                end = c * rows + rows - b * LANES
                value = jnp.where(
                    lane_of(rows) < end, rolled(pieces_ref[c], c * rows - b * LANES), value
                )
            split_into(lhs_ref, g * (GROUP * rows // LANES) + b, value)
        return 0

    lax.fori_loop(0, recv_ref.shape[0] // PACKED // GROUP, group, 0)


def send_rows(sum_ref, send_ref, turned_ref):
    rows = sum_ref.shape[1]

    def group(g, _):
        base = g * (GROUP * rows // LANES)
        for c in range(GROUP):
            b, o = c * rows // LANES, c * rows % LANES
            value = rolled(sum_ref[base + b], -o)
            if o + rows > LANES:
                value = jnp.where(
                    lane_of(rows) < LANES - o, value, rolled(sum_ref[base + b + 1], -o)
                )
            turned_ref[pl.ds(pl.multiple_of((g * GROUP + c) * rows, 8), rows), :] = value
        return 0

    lax.fori_loop(0, turned_ref.shape[0] // rows // GROUP, group, 0)

    def one(d, _):
        put(send_ref, d, turned_ref[pl.ds(pl.multiple_of(d * rows, 8), rows), :])
        return 0

    lax.fori_loop(0, send_ref.shape[0] // PACKED, one, 0, unroll=16)


def operate(lists, weights_ref, lhs_ref, products_ref, sum_ref):
    blocks, rows, _ = sum_ref.shape
    tile_count = products_ref.shape[0] // blocks
    numbers_ref, signs_ref = lists.wait()

    def multiply(n, _):
        at = pl.ds(pl.multiple_of(n * 2 * LANES, 2 * LANES), 2 * LANES)
        both = jnp.dot(lhs_ref[...], weights_ref[:, at], preferred_element_type=f32)
        for j in range(blocks):
            for half in range(2):
                products_ref[j * tile_count + 2 * n + half] = both[
                    j * rows : (j + 1) * rows, half * LANES : (half + 1) * LANES
                ]
        return 0

    lax.fori_loop(0, tile_count // 2, multiply, 0)
    slots = signs_ref.shape[0]

    def run(q, _):
        added = []
        for r in range(TOGETHER):
            at = (q * TOGETHER + r) * RUN
            total = signs_ref[at] * products_ref[numbers_ref[at]]
            for u in range(1, RUN):
                total = total + signs_ref[at + u] * products_ref[numbers_ref[at + u]]
            added.append(total)
        for r in range(TOGETHER):
            sum_ref[numbers_ref[slots + q * TOGETHER + r]] += added[r]
        return 0

    runs = numbers_ref[slots + slots // RUN]
    lax.fori_loop(0, (runs + TOGETHER - 1) // TOGETHER, run, 0)


def runs_of(block_codes, blocks, tile_count):
    row, column, tile, sign = (block_codes[:, field] for field in range(4))
    words = ((column * tile_count + tile) * blocks + row) * 4 + jnp.where(sign > 0, 1, 2)
    listed = row.shape[1]
    slots = (listed + blocks * (RUN - 1) + (TOGETHER - 1) * RUN + 127) // 128 * 128
    at = jnp.arange(listed, dtype=jnp.int32)
    block = jnp.arange(blocks, dtype=jnp.int32)
    within = jnp.sum(
        (row[:, None, :] == row[:, :, None]) & (at[None, None, :] < at[None, :, None]),
        axis=2,
        dtype=jnp.int32,
    )
    counts = jnp.sum(row[:, None, :] == block[None, :, None], axis=2, dtype=jnp.int32)
    runs = (counts + RUN - 1) // RUN
    begin = jnp.sum(jnp.where(block[None, None, :] < row[:, :, None], runs[:, None, :], 0), axis=2)
    place = begin * RUN + within
    slot = jnp.arange(slots, dtype=jnp.int32)
    grouped = jnp.sum(
        jnp.where(place[:, None, :] == slot[None, :, None], words[:, None, :], 0), axis=2
    )
    signs = ((grouped & 1) - ((grouped >> 1) & 1)).astype(f32)
    pair = grouped >> 2
    targets = (pair % blocks).reshape(pair.shape[0], slots // RUN, RUN)[:, :, 0]
    all_runs = jnp.sum(runs, axis=1, keepdims=True)
    numbers = jnp.concatenate([pair // blocks, targets, all_runs], axis=1)
    numbers = jnp.pad(numbers, ((0, 0), (0, -numbers.shape[1] % LANES)))
    return numbers.astype(jnp.int32), signs


class Lists:
    def __init__(self, which_op, given, held, sems):
        self.held = held
        self.copies = [
            pltpu.make_async_copy(source.at[which_op], target, sems.at[at])
            for at, (source, target) in enumerate(zip(given, held))
        ]
        for copy in self.copies:
            copy.start()

    def wait(self):
        for copy in self.copies:
            copy.wait()
        return self.held


def columns(ref, j):
    return ref[:, pl.ds(pl.multiple_of(j * LANES, LANES), LANES)]


def format_kernel(c_ref, o_ref, held_ref, sems, turned_ref, *buffer):
    parts = sems.shape[0]
    width = c_ref.shape[1] // parts
    copies = [
        pltpu.make_async_copy(
            c_ref.at[:, part * width : (part + 1) * width],
            held_ref.at[:, part * width : (part + 1) * width],
            sems.at[part],
        )
        for part in range(parts)
    ]
    for copy in copies:
        copy.start()
    rows = held_ref.shape[0]
    for part in range(parts):
        copies[part].wait()
        for j in range(part * width // LANES, (part + 1) * width // LANES):
            lanes = slice(j * LANES, (j + 1) * LANES)
            turned_ref[lanes, 0:rows] = held_ref[:, lanes].T
    send_turned((o_ref, *buffer), turned_ref)


def weights_kernel(tiles_ref, *weights_refs):
    for k, weights_ref in enumerate(weights_refs):

        def one(t, _):
            tile = tiles_ref[k, t].T
            high = tile.astype(bf16)
            low = (tile - high.astype(f32)).astype(bf16)
            lanes = pl.ds(pl.multiple_of(t * LANES, LANES), LANES)
            weights_ref[0:128, lanes] = high
            weights_ref[128:256, lanes] = high
            weights_ref[256:384, lanes] = low
            return 0

        lax.fori_loop(0, tiles_ref.shape[1], one, 0, unroll=2)


def split_all(c_ref, lhs_ref):
    def one(j, _):
        split_into(lhs_ref, j, columns(c_ref, j))
        return 0

    lax.fori_loop(0, c_ref.shape[1] // LANES, one, 0, unroll=4)


def beta_kernel(n_ref, s_ref, c_ref, w_ref, sum_ref, *work):
    lhs_ref, products_ref, weights_ref, sem, numbers_ref, signs_ref, sems = work
    fetch = pltpu.make_async_copy(w_ref, weights_ref, sem)
    fetch.start()
    lists = Lists(0, (n_ref, s_ref), (numbers_ref, signs_ref), sems)
    split_all(c_ref, lhs_ref)
    fetch.wait()
    sum_ref[...] = jnp.zeros_like(sum_ref)
    operate(lists, weights_ref, lhs_ref, products_ref, sum_ref)


def mixed_kernel(n_ref, s_ref, c_ref, w_ref, o_ref, *work):
    lhs_ref, products_ref, weights_ref, sem, numbers_ref, signs_ref, sems, *rest = work
    sum_ref, turned_ref, *buffer = rest
    fetch = pltpu.make_async_copy(w_ref, weights_ref, sem)
    fetch.start()
    lists = Lists(3, (n_ref, s_ref), (numbers_ref, signs_ref), sems)
    split_all(c_ref, lhs_ref)
    fetch.wait()
    sum_ref[...] = jnp.zeros_like(sum_ref)
    operate(lists, weights_ref, lhs_ref, products_ref, sum_ref)
    send_transposed(lambda j: sum_ref[j], sum_ref.shape[0], (o_ref, *buffer), turned_ref)


def alpha_kernel(n_ref, s_ref, recv_ref, w_ref, sum_ref, *work):
    lhs_ref, products_ref, weights_ref, sem, numbers_ref, signs_ref, sems, pieces_ref = work
    fetch = pltpu.make_async_copy(w_ref, weights_ref, sem)
    fetch.start()
    lists = Lists(1, (n_ref, s_ref), (numbers_ref, signs_ref), sems)
    receive_rows(recv_ref, pieces_ref, lhs_ref)
    fetch.wait()
    sum_ref[...] = jnp.zeros_like(sum_ref)
    operate(lists, weights_ref, lhs_ref, products_ref, sum_ref)


def cross_kernel(n_ref, s_ref, recv_ref, w_ref, alpha_ref, send_ref, *work):
    lhs_ref, products_ref, weights_ref, sem, numbers_ref, signs_ref, sems, *rest = work
    pieces_ref, sum_ref, own_sem, turned_ref = rest
    fetch = pltpu.make_async_copy(w_ref, weights_ref, sem)
    fetch.start()
    fetch_own = pltpu.make_async_copy(alpha_ref, sum_ref, own_sem)
    fetch_own.start()
    lists = Lists(2, (n_ref, s_ref), (numbers_ref, signs_ref), sems)
    receive_rows(recv_ref, pieces_ref, lhs_ref)
    fetch.wait()
    fetch_own.wait()
    operate(lists, weights_ref, lhs_ref, products_ref, sum_ref)
    send_rows(sum_ref, send_ref, turned_ref)


def final_kernel(recv_ref, b_ref, o_ref, turned_ref, beta_ref, sem, out_ref, sems):
    rows = out_ref.shape[0]
    fetch = pltpu.make_async_copy(b_ref, beta_ref, sem)
    fetch.start()

    def one(d, _):
        turned_ref[pl.ds(pl.multiple_of(d * rows, 8), rows), :] = get(recv_ref, d)
        return 0

    lax.fori_loop(0, recv_ref.shape[0] // PACKED, one, 0, unroll=16)
    fetch.wait()
    parts = sems.shape[0]
    width = out_ref.shape[1] // parts
    copies = []
    for part in range(parts):
        for j in range(part * width // LANES, (part + 1) * width // LANES):
            lanes = slice(j * LANES, (j + 1) * LANES)
            out_ref[:, lanes] = turned_ref[lanes, :].T[0:rows] + beta_ref[j]
        at = slice(part * width, (part + 1) * width)
        copies.append(pltpu.make_async_copy(out_ref.at[:, at], o_ref.at[:, at], sems.at[part]))
        copies[-1].start()
    for copy in copies:
        copy.wait()


def call(kernel, out, scratch, operands, flops, held=(), out_space=VMEM, room=52):
    specs = [
        pl.BlockSpec(memory_space=VMEM if at in held else pl.ANY) for at, x in enumerate(operands)
    ]
    moved = sum(x.size * x.dtype.itemsize for x in operands)
    return pl.pallas_call(
        kernel,
        out_shape=out,
        in_specs=specs,
        out_specs=jax.tree.map(lambda _: pl.BlockSpec(memory_space=out_space), out),
        scratch_shapes=scratch,
        compiler_params=pltpu.CompilerParams(vmem_limit_bytes=room << 20),
        cost_estimate=pl.CostEstimate(flops=flops, bytes_accessed=moved, transcendentals=0),
    )(*operands)


def steps(coefficients, block_codes, tile_bank):
    shards = lax.axis_size("rows")
    irreps = lax.axis_size("irrep")
    own, codes, tiles = coefficients[0], block_codes[0], tile_bank[0]
    rows, width = own.shape
    blocks, tile_count = width // LANES, tiles.shape[1]
    flops = 6 * rows * blocks * LANES * LANES * tile_count

    packed = jax.ShapeDtypeStruct((shards * PACKED, LANES), f32)
    summed = jax.ShapeDtypeStruct((blocks, rows, LANES), f32)
    weights = jax.ShapeDtypeStruct((3 * LANES, tile_count * LANES), bf16)
    numbers, signs = runs_of(codes, blocks, tile_count)
    turned = VMEM((width, LANES), f32)
    pieces = VMEM((GROUP, rows, LANES), f32)
    total = VMEM((blocks, rows, LANES), f32)
    whole = VMEM((rows, width), f32)
    dma = pltpu.SemaphoreType.DMA
    parts = 5
    buffer = [VMEM(packed.shape, f32), dma((2,))]
    work = [
        VMEM((blocks * rows, 3 * LANES), bf16),
        VMEM((blocks * tile_count, rows, LANES), f32),
        VMEM(weights.shape, bf16),
        dma,
        SMEM(numbers.shape[1:], jnp.int32),
        SMEM(signs.shape[1:], f32),
        dma((2,)),
    ]

    def exchange(x):
        x = x.reshape(shards, PACKED // 2, 2, LANES)
        x = lax.all_to_all(x, "rows", split_axis=0, concat_axis=0, tiled=True)
        return x.reshape(shards * PACKED, LANES)

    partner = lax.ppermute(own, "irrep", [(i, i ^ irreps // 2) for i in range(irreps)])
    formatted = call(
        format_kernel,
        packed,
        [whole, dma((parts,)), turned, *buffer],
        (own,),
        1 << 20,
        out_space=pl.ANY,
        room=60,
    )
    columns_in = exchange(formatted)
    w0, w1, w2, w3 = call(weights_kernel, [weights] * tiles.shape[0], [], (tiles,), 1 << 20, (0,))
    lists = (numbers, signs)
    mixed = call(
        mixed_kernel,
        packed,
        [*work, total, turned, *buffer],
        (*lists, partner, w3),
        flops,
        (2,),
        pl.ANY,
    )
    cross_in = exchange(mixed)
    beta = call(beta_kernel, summed, work, (*lists, own, w0), flops, (2,))
    alpha = call(alpha_kernel, summed, [*work, pieces], (*lists, columns_in, w1), flops, (2,))
    cross = call(
        cross_kernel,
        packed,
        [*work, pieces, total, dma, turned],
        (*lists, cross_in, w2, alpha),
        flops,
        (2,),
    )
    returned = exchange(cross)
    out = call(
        final_kernel,
        jax.ShapeDtypeStruct((rows, width), f32),
        [turned, total, dma, whole, dma((parts,))],
        (returned, beta),
        1 << 20,
        (0,),
        pl.ANY,
    )
    return out[None]


def solution(mesh):
    in_specs = (
        P("irrep", "rows", None),
        P("irrep", None, None, None),
        P("irrep", None, None, None, None),
    )
    out_specs = P("irrep", "rows", None)
    return jax.shard_map(steps, mesh=mesh, in_specs=in_specs, out_specs=out_specs, check_vma=False)
```

```python
import jax
import jax.numpy as jnp
from jax import lax
from jax.experimental import pallas as pl
from jax.experimental.pallas import tpu as pltpu
from jax.sharding import PartitionSpec as P


LANES = 128
PACKED = 50
GROUP = 8
RUN = 8
TOGETHER = 2
f32, bf16 = jnp.float32, jnp.bfloat16
VMEM, SMEM = pltpu.VMEM, pltpu.SMEM


def lane_of(rows):
    return lax.broadcasted_iota(jnp.int32, (rows, LANES), 1)


def rolled(value, shift):
    shift %= LANES
    return value if shift == 0 else pltpu.roll(value, shift, 1)


CORNER = 16


def sublane():
    return lax.broadcasted_iota(jnp.int32, (8, LANES), 0)


def put(send_ref, d, z):
    by32, by64, by80 = rolled(z[48:64], 32), rolled(z[64:80], 64), rolled(z[48:80], 80)
    send_ref[pl.ds(d * PACKED, 32), :] = jnp.where(lane_of(32) < 80, z[0:32], by80)
    send_ref[pl.ds(d * PACKED + 32, 16), :] = jnp.where(
        lane_of(16) < 80, z[32:48], jnp.where(lane_of(16) < 112, by32, by64)
    )
    lane = lane_of(8)
    corner = jnp.where(lane < 16, by64[0:8], by80[24:32])
    corner = jnp.where(lane < 32, corner, rolled(pltpu.roll(corner, 4, 0), 32))
    corner = jnp.where(lane < 64, corner, rolled(pltpu.roll(corner, 6, 0), 64))
    send_ref[pl.ds(d * PACKED + 48, 2), :] = corner[0:2]


def get(recv_ref, s):
    p = recv_ref[pl.ds(s * PACKED, 48), :]
    by48 = rolled(p[0:32], 48)
    rows48 = jnp.where(lane_of(16) < 48, by48[0:16], rolled(p[32:48], 96))
    tail = rolled(p[32:48], 64)
    two = recv_ref[pl.ds(s * PACKED + 48, 2), :]
    corner = jnp.concatenate([two, two, two, two], axis=0)
    lane = lane_of(8)
    corner = jnp.where(sublane() & 2 > 0, rolled(corner, 64), corner)
    corner = jnp.where(sublane() & 4 > 0, rolled(corner, 96), corner)
    last = []
    for a in range(2):
        at = slice(8 * a, 8 * a + 8)
        last.append(
            jnp.where(
                lane < 48,
                by48[16 + 8 * a : 24 + 8 * a],
                jnp.where(lane < 64, tail[at], rolled(corner, 64 - CORNER * a)),
            )
        )
    return jnp.concatenate([p[0:48], rows48, *last], axis=0)


def send_transposed(tile_at, count, out, turned_ref):
    rows = turned_ref.shape[0] * PACKED // out[1].shape[0]

    def turn(j, _):
        turned_ref[pl.ds(pl.multiple_of(j * LANES, LANES), LANES), 0:rows] = tile_at(j).T
        return 0

    lax.fori_loop(0, count, turn, 0, unroll=10)
    send_turned(out, turned_ref)


def send_turned(out, turned_ref):
    o_ref, send_ref, sems = out
    halves = sems.shape[0]
    shards = send_ref.shape[0] // PACKED
    rows = turned_ref.shape[0] // shards
    each = shards // halves

    def copy_of(h):
        at = pl.ds(pl.multiple_of(h * each * PACKED, 8), each * PACKED)
        return pltpu.make_async_copy(send_ref.at[at], o_ref.at[at], sems.at[h])

    def half(h, _):
        for c in range(each):
            d = h * each + c
            put(send_ref, d, turned_ref[pl.ds(pl.multiple_of(d * rows, 8), rows), :])
        copy_of(h).start()
        return 0

    lax.fori_loop(0, halves, half, 0)
    for h in range(halves):
        copy_of(h).wait()


def split_into(lhs_ref, j, value):
    rows = value.shape[0]
    high = value.astype(bf16)
    low = (value - high.astype(f32)).astype(bf16)
    at = pl.ds(pl.multiple_of(j * rows, 16), rows)
    lhs_ref[at, 0:128] = high
    lhs_ref[at, 128:256] = low
    lhs_ref[at, 256:384] = high


def receive_rows(recv_ref, pieces_ref, lhs_ref):
    rows = pieces_ref.shape[1]

    def group(g, _):
        for c in range(GROUP):
            pieces_ref[c] = get(recv_ref, g * GROUP + c)
        for b in range(GROUP * rows // LANES):
            first, last = b * LANES // rows, (b * LANES + LANES - 1) // rows
            value = rolled(pieces_ref[last], last * rows - b * LANES)
            for c in range(last - 1, first - 1, -1):
                end = c * rows + rows - b * LANES
                value = jnp.where(
                    lane_of(rows) < end, rolled(pieces_ref[c], c * rows - b * LANES), value
                )
            split_into(lhs_ref, g * (GROUP * rows // LANES) + b, value)
        return 0

    lax.fori_loop(0, recv_ref.shape[0] // PACKED // GROUP, group, 0)


def send_rows(sum_ref, send_ref, turned_ref):
    rows = sum_ref.shape[1]

    def group(g, _):
        base = g * (GROUP * rows // LANES)
        for c in range(GROUP):
            b, o = c * rows // LANES, c * rows % LANES
            value = rolled(sum_ref[base + b], -o)
            if o + rows > LANES:
                value = jnp.where(
                    lane_of(rows) < LANES - o, value, rolled(sum_ref[base + b + 1], -o)
                )
            turned_ref[pl.ds(pl.multiple_of((g * GROUP + c) * rows, 8), rows), :] = value
        return 0

    lax.fori_loop(0, turned_ref.shape[0] // rows // GROUP, group, 0)

    def one(d, _):
        put(send_ref, d, turned_ref[pl.ds(pl.multiple_of(d * rows, 8), rows), :])
        return 0

    lax.fori_loop(0, send_ref.shape[0] // PACKED, one, 0, unroll=16)


def operate(lists, weights_ref, lhs_ref, products_ref, sum_ref):
    blocks, rows, _ = sum_ref.shape
    tile_count = products_ref.shape[0] // blocks
    numbers_ref, signs_ref = lists.wait()

    def multiply(n, _):
        at = pl.ds(pl.multiple_of(n * 2 * LANES, 2 * LANES), 2 * LANES)
        both = jnp.dot(lhs_ref[...], weights_ref[:, at], preferred_element_type=f32)
        for j in range(blocks):
            for half in range(2):
                products_ref[j * tile_count + 2 * n + half] = both[
                    j * rows : (j + 1) * rows, half * LANES : (half + 1) * LANES
                ]
        return 0

    lax.fori_loop(0, tile_count // 2, multiply, 0)
    slots = signs_ref.shape[0]

    def run(q, _):
        added = []
        for r in range(TOGETHER):
            at = (q * TOGETHER + r) * RUN
            total = signs_ref[at] * products_ref[numbers_ref[at]]
            for u in range(1, RUN):
                total = total + signs_ref[at + u] * products_ref[numbers_ref[at + u]]
            added.append(total)
        for r in range(TOGETHER):
            sum_ref[numbers_ref[slots + q * TOGETHER + r]] += added[r]
        return 0

    runs = numbers_ref[slots + slots // RUN]
    lax.fori_loop(0, (runs + TOGETHER - 1) // TOGETHER, run, 0)


def runs_of(block_codes, blocks, tile_count):
    row, column, tile, sign = (block_codes[:, field] for field in range(4))
    words = ((column * tile_count + tile) * blocks + row) * 4 + jnp.where(sign > 0, 1, 2)
    listed = row.shape[1]
    slots = (listed + blocks * (RUN - 1) + (TOGETHER - 1) * RUN + 127) // 128 * 128
    at = jnp.arange(listed, dtype=jnp.int32)
    block = jnp.arange(blocks, dtype=jnp.int32)
    within = jnp.sum(
        (row[:, None, :] == row[:, :, None]) & (at[None, None, :] < at[None, :, None]),
        axis=2,
        dtype=jnp.int32,
    )
    counts = jnp.sum(row[:, None, :] == block[None, :, None], axis=2, dtype=jnp.int32)
    runs = (counts + RUN - 1) // RUN
    begin = jnp.sum(jnp.where(block[None, None, :] < row[:, :, None], runs[:, None, :], 0), axis=2)
    place = begin * RUN + within
    slot = jnp.arange(slots, dtype=jnp.int32)
    grouped = jnp.sum(
        jnp.where(place[:, None, :] == slot[None, :, None], words[:, None, :], 0), axis=2
    )
    signs = ((grouped & 1) - ((grouped >> 1) & 1)).astype(f32)
    pair = grouped >> 2
    targets = (pair % blocks).reshape(pair.shape[0], slots // RUN, RUN)[:, :, 0]
    all_runs = jnp.sum(runs, axis=1, keepdims=True)
    numbers = jnp.concatenate([pair // blocks, targets, all_runs], axis=1)
    numbers = jnp.pad(numbers, ((0, 0), (0, -numbers.shape[1] % LANES)))
    return numbers.astype(jnp.int32), signs


class Lists:
    def __init__(self, which_op, given, held, sems):
        self.held = held
        self.copies = [
            pltpu.make_async_copy(source.at[which_op], target, sems.at[at])
            for at, (source, target) in enumerate(zip(given, held))
        ]
        for copy in self.copies:
            copy.start()

    def wait(self):
        for copy in self.copies:
            copy.wait()
        return self.held


def columns(ref, j):
    return ref[:, pl.ds(pl.multiple_of(j * LANES, LANES), LANES)]


def format_kernel(c_ref, o_ref, held_ref, sems, turned_ref, *buffer):
    parts = sems.shape[0]
    width = c_ref.shape[1] // parts
    copies = [
        pltpu.make_async_copy(
            c_ref.at[:, part * width : (part + 1) * width],
            held_ref.at[:, part * width : (part + 1) * width],
            sems.at[part],
        )
        for part in range(parts)
    ]
    for copy in copies:
        copy.start()
    rows = held_ref.shape[0]
    for part in range(parts):
        copies[part].wait()
        for j in range(part * width // LANES, (part + 1) * width // LANES):
            lanes = slice(j * LANES, (j + 1) * LANES)
            turned_ref[lanes, 0:rows] = held_ref[:, lanes].T
    send_turned((o_ref, *buffer), turned_ref)


def weights_kernel(tiles_ref, *weights_refs):
    for k, weights_ref in enumerate(weights_refs):

        def one(t, _):
            tile = tiles_ref[k, t].T
            high = tile.astype(bf16)
            low = (tile - high.astype(f32)).astype(bf16)
            lanes = pl.ds(pl.multiple_of(t * LANES, LANES), LANES)
            weights_ref[0:128, lanes] = high
            weights_ref[128:256, lanes] = high
            weights_ref[256:384, lanes] = low
            return 0

        lax.fori_loop(0, tiles_ref.shape[1], one, 0, unroll=2)


def split_all(c_ref, lhs_ref):
    def one(j, _):
        split_into(lhs_ref, j, columns(c_ref, j))
        return 0

    lax.fori_loop(0, c_ref.shape[1] // LANES, one, 0, unroll=4)


def beta_kernel(n_ref, s_ref, c_ref, w_ref, sum_ref, *work):
    lhs_ref, products_ref, weights_ref, sem, numbers_ref, signs_ref, sems = work
    fetch = pltpu.make_async_copy(w_ref, weights_ref, sem)
    fetch.start()
    lists = Lists(0, (n_ref, s_ref), (numbers_ref, signs_ref), sems)
    split_all(c_ref, lhs_ref)
    fetch.wait()
    sum_ref[...] = jnp.zeros_like(sum_ref)
    operate(lists, weights_ref, lhs_ref, products_ref, sum_ref)


def mixed_kernel(n_ref, s_ref, c_ref, w_ref, o_ref, *work):
    lhs_ref, products_ref, weights_ref, sem, numbers_ref, signs_ref, sems, *rest = work
    sum_ref, turned_ref, *buffer = rest
    fetch = pltpu.make_async_copy(w_ref, weights_ref, sem)
    fetch.start()
    lists = Lists(3, (n_ref, s_ref), (numbers_ref, signs_ref), sems)
    split_all(c_ref, lhs_ref)
    fetch.wait()
    sum_ref[...] = jnp.zeros_like(sum_ref)
    operate(lists, weights_ref, lhs_ref, products_ref, sum_ref)
    send_transposed(lambda j: sum_ref[j], sum_ref.shape[0], (o_ref, *buffer), turned_ref)


def alpha_kernel(n_ref, s_ref, recv_ref, w_ref, sum_ref, *work):
    lhs_ref, products_ref, weights_ref, sem, numbers_ref, signs_ref, sems, pieces_ref = work
    fetch = pltpu.make_async_copy(w_ref, weights_ref, sem)
    fetch.start()
    lists = Lists(1, (n_ref, s_ref), (numbers_ref, signs_ref), sems)
    receive_rows(recv_ref, pieces_ref, lhs_ref)
    fetch.wait()
    sum_ref[...] = jnp.zeros_like(sum_ref)
    operate(lists, weights_ref, lhs_ref, products_ref, sum_ref)


def cross_kernel(n_ref, s_ref, recv_ref, w_ref, alpha_ref, send_ref, *work):
    lhs_ref, products_ref, weights_ref, sem, numbers_ref, signs_ref, sems, *rest = work
    pieces_ref, sum_ref, own_sem, turned_ref = rest
    fetch = pltpu.make_async_copy(w_ref, weights_ref, sem)
    fetch.start()
    fetch_own = pltpu.make_async_copy(alpha_ref, sum_ref, own_sem)
    fetch_own.start()
    lists = Lists(2, (n_ref, s_ref), (numbers_ref, signs_ref), sems)
    receive_rows(recv_ref, pieces_ref, lhs_ref)
    fetch.wait()
    fetch_own.wait()
    operate(lists, weights_ref, lhs_ref, products_ref, sum_ref)
    send_rows(sum_ref, send_ref, turned_ref)


def final_kernel(recv_ref, b_ref, o_ref, turned_ref, beta_ref, sem, out_ref, sems):
    rows = out_ref.shape[0]
    fetch = pltpu.make_async_copy(b_ref, beta_ref, sem)
    fetch.start()

    def one(d, _):
        turned_ref[pl.ds(pl.multiple_of(d * rows, 8), rows), :] = get(recv_ref, d)
        return 0

    lax.fori_loop(0, recv_ref.shape[0] // PACKED, one, 0, unroll=16)
    fetch.wait()
    parts = sems.shape[0]
    width = out_ref.shape[1] // parts
    copies = []
    for part in range(parts):
        for j in range(part * width // LANES, (part + 1) * width // LANES):
            lanes = slice(j * LANES, (j + 1) * LANES)
            out_ref[:, lanes] = turned_ref[lanes, :].T[0:rows] + beta_ref[j]
        at = slice(part * width, (part + 1) * width)
        copies.append(pltpu.make_async_copy(out_ref.at[:, at], o_ref.at[:, at], sems.at[part]))
        copies[-1].start()
    for copy in copies:
        copy.wait()


def call(kernel, out, scratch, operands, flops, held=(), out_space=VMEM, room=52):
    specs = [
        pl.BlockSpec(memory_space=VMEM if at in held else pl.ANY) for at, x in enumerate(operands)
    ]
    moved = sum(x.size * x.dtype.itemsize for x in operands)
    return pl.pallas_call(
        kernel,
        out_shape=out,
        in_specs=specs,
        out_specs=jax.tree.map(lambda _: pl.BlockSpec(memory_space=out_space), out),
        scratch_shapes=scratch,
        compiler_params=pltpu.CompilerParams(vmem_limit_bytes=room << 20),
        cost_estimate=pl.CostEstimate(flops=flops, bytes_accessed=moved, transcendentals=0),
    )(*operands)


def steps(coefficients, block_codes, tile_bank):
    shards = lax.axis_size("rows")
    irreps = lax.axis_size("irrep")
    own, codes, tiles = coefficients[0], block_codes[0], tile_bank[0]
    rows, width = own.shape
    blocks, tile_count = width // LANES, tiles.shape[1]
    flops = 6 * rows * blocks * LANES * LANES * tile_count

    packed = jax.ShapeDtypeStruct((shards * PACKED, LANES), f32)
    summed = jax.ShapeDtypeStruct((blocks, rows, LANES), f32)
    weights = jax.ShapeDtypeStruct((3 * LANES, tile_count * LANES), bf16)
    numbers, signs = runs_of(codes, blocks, tile_count)
    turned = VMEM((width, LANES), f32)
    pieces = VMEM((GROUP, rows, LANES), f32)
    total = VMEM((blocks, rows, LANES), f32)
    whole = VMEM((rows, width), f32)
    dma = pltpu.SemaphoreType.DMA
    parts = 5
    buffer = [VMEM(packed.shape, f32), dma((2,))]
    work = [
        VMEM((blocks * rows, 3 * LANES), bf16),
        VMEM((blocks * tile_count, rows, LANES), f32),
        VMEM(weights.shape, bf16),
        dma,
        SMEM(numbers.shape[1:], jnp.int32),
        SMEM(signs.shape[1:], f32),
        dma((2,)),
    ]

    def exchange(x):
        x = x.reshape(shards, PACKED // 2, 2, LANES)
        x = lax.all_to_all(x, "rows", split_axis=0, concat_axis=0, tiled=True)
        return x.reshape(shards * PACKED, LANES)

    partner = lax.ppermute(own, "irrep", [(i, i ^ irreps // 2) for i in range(irreps)])
    formatted = call(
        format_kernel,
        packed,
        [whole, dma((parts,)), turned, *buffer],
        (own,),
        1 << 20,
        out_space=pl.ANY,
        room=60,
    )
    columns_in = exchange(formatted)
    w0, w1, w2, w3 = call(weights_kernel, [weights] * tiles.shape[0], [], (tiles,), 1 << 20, (0,))
    lists = (numbers, signs)
    mixed = call(
        mixed_kernel,
        packed,
        [*work, total, turned, *buffer],
        (*lists, partner, w3),
        flops,
        (2,),
        pl.ANY,
    )
    cross_in = exchange(mixed)
    beta = call(beta_kernel, summed, work, (*lists, own, w0), flops, (2,), room=52)
    alpha = call(alpha_kernel, summed, [*work, pieces], (*lists, columns_in, w1), flops, (2,), room=51)
    cross = call(
        cross_kernel,
        packed,
        [*work, pieces, total, dma, turned],
        (*lists, cross_in, w2, alpha),
        flops,
        (2,),
        room=51,
    )
    returned = exchange(cross)
    out = call(
        final_kernel,
        jax.ShapeDtypeStruct((rows, width), f32),
        [turned, total, dma, whole, dma((parts,))],
        (returned, beta),
        1 << 20,
        (0,),
        pl.ANY,
    )
    return out[None]


def solution(mesh):
    in_specs = (
        P("irrep", "rows", None),
        P("irrep", None, None, None),
        P("irrep", None, None, None, None),
    )
    out_specs = P("irrep", "rows", None)
    return jax.shard_map(steps, mesh=mesh, in_specs=in_specs, out_specs=out_specs, check_vma=False)
```
